256 devices in a mesh: rep: 8 (over x, z_lo), mp: 32 (over z_hi, y, core).
Axes of the slice: x: 4, y: 4, z: 8 (z_hi: 4, z_lo: 2; z = z_hi * 2 + z_lo), core: 2. Of those that a mesh axis runs over, the one named last changes fastest.
Arguments:
- tokens: bfloat16 [8, 2048, 5120], P('rep', 'mp'), may hold values from -6 to 6
- prompt_ids: int32 [8, 2048], P('rep', 'mp'), may hold values from 0 to 11, never falling along the last dimension, each value on 1 to 512 neighbouring positions
- modulation: float32 [8, 12, 3, 5120], P('rep'), may hold values from -4 to 4
- trainer_up: float32 [5120, 13824], P('mp', 'rep'), may hold values from -0.078125 to 0.078125
- trainer_down: float32 [13824, 5120], P('rep', 'mp'), may hold values from -0.0546875 to 0.0546875
Outputs:
- result: bfloat16 [8, 2048, 5120], P('rep', 'mp')
The draws below stay inside these ranges and needn't reach their ends.
Inputs may be any that keep to these rules, and one draw needn't show every extreme that they name: `prompt_ids`: along each replica's 2048 tokens the prompt number never falls; each of the 12 prompts has at least one token, and one prompt has exactly a quarter of 2048.
All inputs are finite; a program needn't handle non-finite values.
Results may differ from the reference program's by a relative error of at most 0.023.
Values may be sent and summed in bfloat16 or wider, within the bound.
A program may use at most 192 MiB of HBM per device.

```python
import math
import jax
import jax.numpy as jnp
import numpy as np
from jax import lax

D = 5120
FF = 13824
PROMPTS_REP = 12
T_REP = 2048
N_REP = 8
N_MP = 32


def draw_tokens(key, part):
    key_offset, key_spread, key_base = jax.random.split(key, 3)
    offset = jax.random.uniform(key_offset, (N_REP, T_REP, 1), jnp.float32, -2.0, 2.0)
    spread = jnp.exp(jax.random.uniform(key_spread, (N_REP, T_REP, 1), jnp.float32, math.log(0.35), math.log(1.3)))
    base = jnp.clip(jax.random.normal(key_base, (N_REP, T_REP, D), jnp.float32), -3.0, 3.0)
    values = offset + spread * base
    return values.astype(jnp.bfloat16)


def levels(key, extent, cuts, smallest, high):
    def one(axis_at, blocks):
        draws = jax.random.uniform(jax.random.fold_in(jax.random.fold_in(key, 6), axis_at), (blocks,), jnp.float32, smallest / len(cuts), high / len(cuts))
        return jnp.repeat(jnp.exp(draws), extent[axis_at] // blocks).reshape((-1,) + (1,) * (len(extent) - axis_at - 1))

    loudness = one(*cuts[0])
    for cut in cuts[1:]:
        loudness = loudness * one(*cut)
    return loudness


def split_up(number_of, total, most, slope):
    portions = [(1 << 20) // math.isqrt(rank ** slope) + 1 for rank in range(2, number_of + 1)]
    rest, counts = total - most - (number_of - 1), [1] * (number_of - 1)
    while rest > 0:
        candidates = [i for i in range(number_of - 1) if counts[i] < most]
        mass, left = sum([portions[i] for i in candidates]), rest
        for i in candidates:
            addition = min(most - counts[i], max(1, left * portions[i] // mass), rest)
            counts[i] = counts[i] + addition
            rest = rest - addition
    return np.array([most] + counts)


def uneven(own_key, amount, total, limit, skew):
    if amount == 2:
        one = jax.random.randint(own_key, (), max(1, total - limit), min(limit, total - 1) + 1)
        return jnp.stack([one, total - one])
    lengths = jnp.asarray(split_up(amount, total, limit, skew), jnp.int32)
    twos = (amount - 1) // 2
    source_of, sink = lengths[1:1 + 2 * twos:2], lengths[2:2 + 2 * twos:2]
    room = jnp.minimum(source_of - 1, limit - sink)
    passed = jax.random.randint(jax.random.fold_in(own_key, 1), (twos,), 0, 1 << 20) % (room + 1)
    lengths = lengths.at[1:1 + 2 * twos:2].set(source_of - passed).at[2:2 + 2 * twos:2].set(sink + passed)
    return lengths[jax.random.permutation(jax.random.fold_in(own_key, 2), amount)]


def scatter_about(rng, extent, deviation, reach, cuts=(), kind=jnp.bfloat16):
    values = jax.random.normal(rng, extent, jnp.float32) * deviation
    if len(cuts) > 0:
        values = levels(rng, extent, cuts, -0.22, 0.18) * values
    return jnp.clip(values, min=-reach, max=reach).astype(kind)


def setup_inputs(seed: int = 0) -> dict:
    seeds = jax.random.split(jax.random.key(seed), 6)
    return {
        "tokens": draw_tokens(jax.random.fold_in(seeds[5], 71), 0),
        "prompt_ids": jax.vmap(lambda own: jnp.searchsorted(jnp.cumsum(uneven(own, PROMPTS_REP, T_REP, T_REP // 4, 2)), jnp.arange(T_REP), side="right"))(jax.random.split(seeds[1], N_REP)).reshape((N_REP, T_REP)).astype(jnp.int32),
        "modulation": scatter_about(seeds[2], (N_REP, PROMPTS_REP, 3, D), 0.7, 4.0, ((0, 8),), jnp.float32),
        "trainer_up": scatter_about(seeds[3], (D, FF), D ** -0.5, 0.078125, ((0, 32), (1, 8)), jnp.float32),
        "trainer_down": scatter_about(seeds[4], (FF, D), FF ** -0.5, 0.0546875, ((0, 8), (1, 32)), jnp.float32),
    }


def reference(tokens, prompt_ids, modulation, trainer_up, trainer_down):
    as_float = tokens.astype(jnp.float32)
    average = lax.optimization_barrier(jnp.mean(as_float, axis=-1, keepdims=True))
    centred = as_float - average
    variance = lax.optimization_barrier(jnp.mean(centred * centred, axis=-1, keepdims=True))
    normed = centred / jnp.sqrt(variance + 1e-06)
    onehot = (prompt_ids[:, :, None] == jnp.arange(PROMPTS_REP, dtype=jnp.int32)[None, None, :]).astype(jnp.float32)
    chosen = jnp.einsum('rtp,rpkd->rtkd', onehot, modulation, precision=lax.Precision.HIGHEST)
    shift = chosen[:, :, 0]
    scale = chosen[:, :, 1]
    gate = chosen[:, :, 2]
    xin = (normed * (1.0 + scale) + shift).astype(jnp.bfloat16)
    w_up = trainer_up.astype(jnp.bfloat16)
    w_down = trainer_down.astype(jnp.bfloat16)
    flat = xin.reshape(N_REP * T_REP, D)
    hidden = jax.nn.gelu(jnp.dot(flat, w_up, preferred_element_type=jnp.float32), approximate=True).astype(jnp.bfloat16)
    group = FF // N_MP
    hid_groups = hidden.reshape(N_REP * T_REP, N_MP, group).transpose(1, 0, 2)
    down_groups = w_down.reshape(N_MP, group, D)

    def add_group(index, total):
        partial_sum = jnp.dot(hid_groups[index], down_groups[index], preferred_element_type=jnp.float32).astype(jnp.bfloat16)
        partial_sum = lax.optimization_barrier(partial_sum)
        return total + partial_sum.astype(jnp.float32)
    mlp = lax.fori_loop(0, N_MP, add_group, jnp.zeros((N_REP * T_REP, D), jnp.float32))
    result = as_float + gate * mlp.reshape(N_REP, T_REP, D)
    return result.astype(jnp.bfloat16)
```

```python
import jax
import jax.numpy as jnp
import numpy as np
from jax import lax
from jax.sharding import Mesh, PartitionSpec as P

MP = ("mc", "core")


def local(tokens, prompt_ids, modulation, trainer_up, trainer_down):
    as_float = tokens[0].astype(jnp.float32)
    average = jnp.mean(as_float, axis=-1, keepdims=True)
    centred = as_float - average
    variance = jnp.mean(centred * centred, axis=-1, keepdims=True)
    normed = centred / jnp.sqrt(variance + 1e-06)
    prompts_here = modulation.shape[1]
    onehot = (prompt_ids[0][:, None] == jnp.arange(prompts_here, dtype=jnp.int32)[None, :]).astype(
        jnp.float32
    )
    chosen = jnp.einsum("tp,pkd->tkd", onehot, modulation[0], precision=lax.Precision.HIGHEST)
    shift = chosen[:, 0]
    scale = chosen[:, 1]
    gate = chosen[:, 2]
    xin = (normed * (1.0 + scale) + shift).astype(jnp.bfloat16)

    n_mp = lax.psum(1, MP)
    rows, cols = trainer_up.shape
    piece = cols // n_mp
    up_half = trainer_up.astype(jnp.bfloat16).reshape(rows, n_mp, piece).transpose(1, 0, 2)
    up_cols = lax.all_to_all(up_half, MP, 0, 0, tiled=True).reshape(n_mp * rows, piece)
    up_mine = lax.all_gather(up_cols, "rep", axis=1, tiled=True)
    up_other = lax.ppermute(up_mine, "core", [(0, 1), (1, 0)])
    w_up = jnp.concatenate([up_mine, up_other], axis=1)

    frows, dcols = trainer_down.shape
    down_half = trainer_down.astype(jnp.bfloat16).reshape(n_mp, piece, dcols)
    down_rows = lax.all_to_all(down_half, MP, 0, 0, tiled=True)
    down_rows = down_rows.reshape(n_mp, piece, dcols).transpose(1, 0, 2).reshape(piece, n_mp * dcols)
    down_mine = lax.all_gather(down_rows, "rep", axis=0, tiled=True)
    down_other = lax.ppermute(down_mine, "core", [(0, 1), (1, 0)])
    w_down = jnp.concatenate([down_mine, down_other], axis=0)

    x_all = lax.all_gather(xin, "mc", axis=0, tiled=True)
    hidden = jax.nn.gelu(
        jnp.dot(x_all, w_up, preferred_element_type=jnp.float32), approximate=True
    ).astype(jnp.bfloat16)
    mlp = lax.psum_scatter(
        jnp.dot(hidden, w_down, preferred_element_type=jnp.float32).astype(jnp.bfloat16),
        "mc",
        scatter_dimension=0,
        tiled=True,
    ).astype(jnp.float32)
    result = as_float + gate * mlp
    return result.astype(jnp.bfloat16)[None]


def solution(mesh):
    n_rep, n_mp = mesh.devices.shape
    chips = Mesh(mesh.devices.reshape(n_rep, n_mp // 2, 2), ("rep", "mc", "core"))
    in_specs = (
        P("rep", MP, None),
        P("rep", MP),
        P("rep", None, None, None),
        P(MP, "rep"),
        P("rep", MP),
    )
    out_specs = P("rep", MP, None)
    return jax.shard_map(local, mesh=chips, in_specs=in_specs, out_specs=out_specs, check_vma=False)
```

```python
import functools

import jax
import jax.numpy as jnp
from jax import lax
from jax.experimental import pallas as pl
from jax.experimental.pallas import tpu as pltpu
from jax.sharding import Mesh, PartitionSpec as P

MP = ("mc", "core")
MESH_ID = pl.DeviceIdType.MESH


def handover_kernel(up_ref, dn_ref, up_out, dn_out, send_sem, recv_sem, fwd_send, fwd_recv, local_sem):
    n_rep = up_out.shape[1]
    me = lax.axis_index("rep")
    mc = lax.axis_index("mc")
    c = lax.axis_index("core")
    other = 1 - c

    barrier = pltpu.get_barrier_semaphore()
    for k in range(1, n_rep):
        pl.semaphore_signal(barrier, 1, device_id=(lax.rem(me + k, n_rep), mc, c), device_id_type=MESH_ID)
    pl.semaphore_signal(barrier, 1, device_id=(me, mc, other), device_id_type=MESH_ID)
    pl.semaphore_wait(barrier, n_rep)

    pairs = ((up_ref, up_out), (dn_ref, dn_out))
    locals_ = []
    sends = []
    for i, (src, dst) in enumerate(pairs):
        cp = pltpu.make_async_copy(src, dst.at[c, me], local_sem.at[i])
        cp.start()
        locals_.append(cp)
        for k in range(1, n_rep):
            cp = pltpu.make_async_remote_copy(
                src_ref=src,
                dst_ref=dst.at[c, me],
                send_sem=send_sem.at[i, k],
                recv_sem=recv_sem.at[i, k],
                device_id=(lax.rem(me + k, n_rep), mc, c),
                device_id_type=MESH_ID,
            )
            cp.start()
            sends.append(cp)

    forwards = []
    for i, (src, dst) in enumerate(pairs):
        for k in range(n_rep):
            slot = lax.rem(me + n_rep - k, n_rep)
            if k == 0:
                locals_[i].wait()
            else:
                pltpu.make_async_remote_copy(
                    src_ref=src,
                    dst_ref=dst.at[c, slot],
                    send_sem=send_sem.at[i, k],
                    recv_sem=recv_sem.at[i, k],
                    device_id=(slot, mc, c),
                    device_id_type=MESH_ID,
                ).wait_recv()
            fw = pltpu.make_async_remote_copy(
                src_ref=dst.at[c, slot],
                dst_ref=dst.at[c, slot],
                send_sem=fwd_send.at[i, k],
                recv_sem=fwd_recv.at[i, k],
                device_id=(me, mc, other),
                device_id_type=MESH_ID,
            )
            fw.start()
            forwards.append(fw)

    for cp in sends:
        cp.wait_send()
    for i, (src, dst) in enumerate(pairs):
        for k in range(n_rep):
            slot = lax.rem(me + n_rep - k, n_rep)
            pltpu.make_async_remote_copy(
                src_ref=dst.at[other, slot],
                dst_ref=dst.at[other, slot],
                send_sem=fwd_send.at[i, k],
                recv_sem=fwd_recv.at[i, k],
                device_id=(me, mc, other),
                device_id_type=MESH_ID,
            ).wait_recv()
    for fw in forwards:
        fw.wait_send()


def handover(up_blk, dn_blk, n_rep):
    units, width = up_blk.shape
    shape = jax.ShapeDtypeStruct((2, n_rep, units, width), up_blk.dtype)
    return pl.pallas_call(
        handover_kernel,
        out_shape=(shape, shape),
        in_specs=[pl.BlockSpec(memory_space=pl.ANY)] * 2,
        out_specs=(pl.BlockSpec(memory_space=pl.ANY),) * 2,
        scratch_shapes=[
            pltpu.SemaphoreType.DMA((2, n_rep)),
            pltpu.SemaphoreType.DMA((2, n_rep)),
            pltpu.SemaphoreType.DMA((2, n_rep)),
            pltpu.SemaphoreType.DMA((2, n_rep)),
            pltpu.SemaphoreType.DMA((2,)),
        ],
        compiler_params=pltpu.CompilerParams(collective_id=0, has_side_effects=True),
    )(up_blk, dn_blk)


def local(tokens, prompt_ids, modulation, trainer_up, trainer_down):
    as_float = tokens[0].astype(jnp.float32)
    average = jnp.mean(as_float, axis=-1, keepdims=True)
    centred = as_float - average
    variance = jnp.mean(centred * centred, axis=-1, keepdims=True)
    normed = centred / jnp.sqrt(variance + 1e-06)
    prompts_here = modulation.shape[1]
    onehot = (prompt_ids[0][:, None] == jnp.arange(prompts_here, dtype=jnp.int32)[None, :]).astype(
        jnp.float32
    )
    chosen = jnp.einsum("tp,pkd->tkd", onehot, modulation[0], precision=lax.Precision.HIGHEST)
    shift = chosen[:, 0]
    scale = chosen[:, 1]
    gate = chosen[:, 2]
    xin = (normed * (1.0 + scale) + shift).astype(jnp.bfloat16)
    x_all = lax.all_gather(xin, "mc", axis=0, tiled=True)

    n_mp = lax.psum(1, MP)
    n_rep = lax.psum(1, "rep")
    rows, cols = trainer_up.shape
    piece = cols // n_mp
    both = jnp.stack([trainer_up.astype(jnp.bfloat16).T, trainer_down.astype(jnp.bfloat16)])
    both = lax.all_to_all(both.reshape(2, n_mp, piece, rows), MP, 1, 1, tiled=True)
    both = both.transpose(0, 2, 1, 3).reshape(2, piece, n_mp * rows)
    up_all, dn_all = handover(both[0], both[1], n_rep)
    units = 2 * n_rep * piece
    w_up_t = up_all.reshape(units, n_mp * rows)
    w_down = dn_all.reshape(units, n_mp * rows)

    hidden = jax.nn.gelu(
        lax.dot_general(x_all, w_up_t, (((1,), (1,)), ((), ())), preferred_element_type=jnp.float32),
        approximate=True,
    ).astype(jnp.bfloat16)
    mlp = lax.psum_scatter(
        jnp.dot(hidden, w_down, preferred_element_type=jnp.float32).astype(jnp.bfloat16),
        "mc",
        scatter_dimension=0,
        tiled=True,
    ).astype(jnp.float32)
    result = as_float + gate * mlp
    return result.astype(jnp.bfloat16)[None]


def solution(mesh):
    n_rep, n_mp = mesh.devices.shape
    chips = Mesh(mesh.devices.reshape(n_rep, n_mp // 2, 2), ("rep", "mc", "core"))
    in_specs = (
        P("rep", MP, None),
        P("rep", MP),
        P("rep", None, None, None),
        P(MP, "rep"),
        P("rep", MP),
    )
    out_specs = P("rep", MP, None)
    return jax.shard_map(local, mesh=chips, in_specs=in_specs, out_specs=out_specs, check_vma=False)
```

```python
import functools

import jax
import jax.numpy as jnp
from jax import lax
from jax.experimental import pallas as pl
from jax.experimental.pallas import tpu as pltpu
from jax.sharding import Mesh, PartitionSpec as P

MP = ("mc", "core")
MESH_ID = pl.DeviceIdType.MESH


def exchange_kernel(src, dst, send_sem, recv_sem, local_sem):
    n = src.shape[0]
    me = lax.axis_index("mc") * 2 + lax.axis_index("core")
    r = lax.axis_index("rep")

    def dev(i):
        return (r, lax.div(i, 2), lax.rem(i, 2))

    barrier = pltpu.get_barrier_semaphore()
    for k in range(1, n):
        pl.semaphore_signal(barrier, 1, device_id=dev(lax.rem(me + k, n)), device_id_type=MESH_ID)
    pl.semaphore_wait(barrier, n - 1)
    own = pltpu.make_async_copy(src.at[me], dst.at[me], local_sem.at[0])
    own.start()
    sends = []
    for k in range(1, n):
        t = lax.rem(me + k, n)
        cp = pltpu.make_async_remote_copy(
            src_ref=src.at[t],
            dst_ref=dst.at[me],
            send_sem=send_sem.at[k],
            recv_sem=recv_sem.at[k],
            device_id=dev(t),
            device_id_type=MESH_ID,
        )
        cp.start()
        sends.append(cp)
    for k in range(1, n):
        s = lax.rem(me + n - k, n)
        pltpu.make_async_remote_copy(
            src_ref=src.at[s],
            dst_ref=dst.at[s],
            send_sem=send_sem.at[k],
            recv_sem=recv_sem.at[k],
            device_id=dev(s),
            device_id_type=MESH_ID,
        ).wait_recv()
    for cp in sends:
        cp.wait_send()
    own.wait()


def exchange(pieces):
    n = pieces.shape[0]
    return pl.pallas_call(
        exchange_kernel,
        out_shape=jax.ShapeDtypeStruct(pieces.shape, pieces.dtype),
        in_specs=[pl.BlockSpec(memory_space=pl.ANY)],
        out_specs=pl.BlockSpec(memory_space=pl.ANY),
        scratch_shapes=[
            pltpu.SemaphoreType.DMA((n,)),
            pltpu.SemaphoreType.DMA((n,)),
            pltpu.SemaphoreType.DMA((1,)),
        ],
        compiler_params=pltpu.CompilerParams(collective_id=1, has_side_effects=True),
    )(pieces)


def handover_kernel(up_ref, dn_ref, up_out, dn_out, send_sem, recv_sem, fwd_send, fwd_recv, local_sem):
    n_rep = up_out.shape[1]
    n_x = n_rep // 2
    me = lax.axis_index("rep")
    mc = lax.axis_index("mc")
    c = lax.axis_index("core")
    other = 1 - c
    x = lax.div(me, 2)
    zl = lax.rem(me, 2)
    partner = me + 1 - 2 * zl
    xs = [lax.rem(x + d, n_x) * 2 for d in range(1, n_x)]

    barrier = pltpu.get_barrier_semaphore()
    for t in [partner] + [xo + zl for xo in xs]:
        pl.semaphore_signal(barrier, 1, device_id=(t, mc, c), device_id_type=MESH_ID)
    pl.semaphore_signal(barrier, 1, device_id=(me, mc, other), device_id_type=MESH_ID)
    pl.semaphore_wait(barrier, n_x + 1)

    pairs = ((up_ref, up_out), (dn_ref, dn_out))

    def recv_desc(i, slot):
        dst = pairs[i][1]
        return pltpu.make_async_remote_copy(
            src_ref=dst.at[c, slot],
            dst_ref=dst.at[c, slot],
            send_sem=send_sem.at[i, 0],
            recv_sem=recv_sem.at[i, slot],
            device_id=(slot, mc, c),
            device_id_type=MESH_ID,
        )

    locals_ = []
    sends = []
    for i, (src, dst) in enumerate(pairs):
        cp = pltpu.make_async_copy(src, dst.at[c, me], local_sem.at[i])
        cp.start()
        locals_.append(cp)
        for j, t in enumerate([partner] + [xo + zl for xo in xs]):
            cp = pltpu.make_async_remote_copy(
                src_ref=src,
                dst_ref=dst.at[c, me],
                send_sem=send_sem.at[i, j],
                recv_sem=recv_sem.at[i, me],
                device_id=(t, mc, c),
                device_id_type=MESH_ID,
            )
            cp.start()
            sends.append(cp)
    for i, (src, dst) in enumerate(pairs):
        recv_desc(i, partner).wait_recv()
        for j, xo in enumerate(xs):
            cp = pltpu.make_async_remote_copy(
                src_ref=dst.at[c, partner],
                dst_ref=dst.at[c, partner],
                send_sem=send_sem.at[i, n_x + j],
                recv_sem=recv_sem.at[i, partner],
                device_id=(xo + zl, mc, c),
                device_id_type=MESH_ID,
            )
            cp.start()
            sends.append(cp)

    forwards = []
    for i, (src, dst) in enumerate(pairs):
        order = [me, partner] + [xo + zl for xo in xs] + [xo + 1 - zl for xo in xs]
        for slot in order:
            if slot is me:
                locals_[i].wait()
            elif slot is not partner:
                recv_desc(i, slot).wait_recv()
            fw = pltpu.make_async_remote_copy(
                src_ref=dst.at[c, slot],
                dst_ref=dst.at[c, slot],
                send_sem=fwd_send.at[i, slot],
                recv_sem=fwd_recv.at[i, slot],
                device_id=(me, mc, other),
                device_id_type=MESH_ID,
            )
            fw.start()
            forwards.append(fw)

    for cp in sends:
        cp.wait_send()
    for i, (src, dst) in enumerate(pairs):
        for slot in range(n_rep):
            pltpu.make_async_remote_copy(
                src_ref=dst.at[other, slot],
                dst_ref=dst.at[other, slot],
                send_sem=fwd_send.at[i, slot],
                recv_sem=fwd_recv.at[i, slot],
                device_id=(me, mc, other),
                device_id_type=MESH_ID,
            ).wait_recv()
    for fw in forwards:
        fw.wait_send()


def handover(up_blk, dn_blk, n_rep):
    units, width = up_blk.shape
    shape = jax.ShapeDtypeStruct((2, n_rep, units, width), up_blk.dtype)
    return pl.pallas_call(
        handover_kernel,
        out_shape=(shape, shape),
        in_specs=[pl.BlockSpec(memory_space=pl.ANY)] * 2,
        out_specs=(pl.BlockSpec(memory_space=pl.ANY),) * 2,
        scratch_shapes=[
            pltpu.SemaphoreType.DMA((2, n_rep)),
            pltpu.SemaphoreType.DMA((2, n_rep)),
            pltpu.SemaphoreType.DMA((2, n_rep)),
            pltpu.SemaphoreType.DMA((2, n_rep)),
            pltpu.SemaphoreType.DMA((2,)),
        ],
        compiler_params=pltpu.CompilerParams(collective_id=0, has_side_effects=True),
    )(up_blk, dn_blk)


def local(tokens, prompt_ids, modulation, trainer_up, trainer_down):
    as_float = tokens[0].astype(jnp.float32)
    average = jnp.mean(as_float, axis=-1, keepdims=True)
    centred = as_float - average
    variance = jnp.mean(centred * centred, axis=-1, keepdims=True)
    normed = centred / jnp.sqrt(variance + 1e-06)
    prompts_here = modulation.shape[1]
    onehot = (prompt_ids[0][:, None] == jnp.arange(prompts_here, dtype=jnp.int32)[None, :]).astype(
        jnp.float32
    )
    chosen = jnp.einsum("tp,pkd->tkd", onehot, modulation[0], precision=lax.Precision.HIGHEST)
    shift = chosen[:, 0]
    scale = chosen[:, 1]
    gate = chosen[:, 2]
    xin = (normed * (1.0 + scale) + shift).astype(jnp.bfloat16)
    x_all = lax.all_gather(xin, "mc", axis=0, tiled=True)

    n_mp = lax.psum(1, MP)
    n_rep = lax.psum(1, "rep")
    rows, cols = trainer_up.shape
    piece = cols // n_mp
    both = jnp.stack([trainer_up.astype(jnp.bfloat16).T, trainer_down.astype(jnp.bfloat16)])
    both = exchange(both.reshape(2, n_mp, piece, rows).transpose(1, 0, 2, 3))
    both = both.transpose(1, 2, 0, 3).reshape(2, piece, n_mp * rows)
    up_all, dn_all = handover(both[0], both[1], n_rep)
    units = 2 * n_rep * piece
    w_up_t = up_all.reshape(units, n_mp * rows)
    w_down = dn_all.reshape(units, n_mp * rows)

    hidden = jax.nn.gelu(
        lax.dot_general(x_all, w_up_t, (((1,), (1,)), ((), ())), preferred_element_type=jnp.float32),
        approximate=True,
    ).astype(jnp.bfloat16)
    mlp = lax.psum_scatter(
        jnp.dot(hidden, w_down, preferred_element_type=jnp.float32).astype(jnp.bfloat16),
        "mc",
        scatter_dimension=0,
        tiled=True,
    ).astype(jnp.float32)
    result = as_float + gate * mlp
    return result.astype(jnp.bfloat16)[None]


def solution(mesh):
    n_rep, n_mp = mesh.devices.shape
    chips = Mesh(mesh.devices.reshape(n_rep, n_mp // 2, 2), ("rep", "mc", "core"))
    in_specs = (
        P("rep", MP, None),
        P("rep", MP),
        P("rep", None, None, None),
        P(MP, "rep"),
        P("rep", MP),
    )
    out_specs = P("rep", MP, None)
    return jax.shard_map(local, mesh=chips, in_specs=in_specs, out_specs=out_specs, check_vma=False)
```

```python
import functools

import jax
import jax.numpy as jnp
from jax import lax
from jax.experimental import pallas as pl
from jax.experimental.pallas import tpu as pltpu
from jax.sharding import Mesh, PartitionSpec as P

MP = ("mc", "core")
MESH_ID = pl.DeviceIdType.MESH


def exchange_kernel(src, dst, send_sem, recv_sem, local_sem):
    n = src.shape[0]
    me = lax.axis_index("mc") * 2 + lax.axis_index("core")
    r = lax.axis_index("rep")

    def dev(i):
        return (r, lax.div(i, 2), lax.rem(i, 2))

    barrier = pltpu.get_barrier_semaphore()
    for k in range(1, n):
        pl.semaphore_signal(barrier, 1, device_id=dev(lax.rem(me + k, n)), device_id_type=MESH_ID)
    pl.semaphore_wait(barrier, n - 1)
    own = pltpu.make_async_copy(src.at[me], dst.at[me], local_sem.at[0])
    own.start()
    sends = []
    for k in range(1, n):
        t = lax.rem(me + k, n)
        cp = pltpu.make_async_remote_copy(
            src_ref=src.at[t],
            dst_ref=dst.at[me],
            send_sem=send_sem.at[k],
            recv_sem=recv_sem.at[k],
            device_id=dev(t),
            device_id_type=MESH_ID,
        )
        cp.start()
        sends.append(cp)
    for k in range(1, n):
        s = lax.rem(me + n - k, n)
        pltpu.make_async_remote_copy(
            src_ref=src.at[s],
            dst_ref=dst.at[s],
            send_sem=send_sem.at[k],
            recv_sem=recv_sem.at[k],
            device_id=dev(s),
            device_id_type=MESH_ID,
        ).wait_recv()
    for cp in sends:
        cp.wait_send()
    own.wait()


def exchange(pieces):
    n = pieces.shape[0]
    return pl.pallas_call(
        exchange_kernel,
        out_shape=jax.ShapeDtypeStruct(pieces.shape, pieces.dtype),
        in_specs=[pl.BlockSpec(memory_space=pl.ANY)],
        out_specs=pl.BlockSpec(memory_space=pl.ANY),
        scratch_shapes=[
            pltpu.SemaphoreType.DMA((n,)),
            pltpu.SemaphoreType.DMA((n,)),
            pltpu.SemaphoreType.DMA((1,)),
        ],
        compiler_params=pltpu.CompilerParams(collective_id=1, has_side_effects=True),
    )(pieces)


def handover_kernel(up_ref, dn_ref, up_out, dn_out, send_sem, recv_sem, fwd_send, fwd_recv, local_sem):
    n_rep = up_out.shape[1]
    n_x = n_rep // 2
    me = lax.axis_index("rep")
    mc = lax.axis_index("mc")
    c = lax.axis_index("core")
    other = 1 - c
    x = lax.div(me, 2)
    zl = lax.rem(me, 2)
    partner = me + 1 - 2 * zl
    xs = [lax.rem(x + d, n_x) * 2 for d in range(1, n_x)]

    barrier = pltpu.get_barrier_semaphore()
    for t in [partner] + [xo + zl for xo in xs]:
        pl.semaphore_signal(barrier, 1, device_id=(t, mc, c), device_id_type=MESH_ID)
    pl.semaphore_signal(barrier, 1, device_id=(me, mc, other), device_id_type=MESH_ID)
    pl.semaphore_wait(barrier, n_x + 1)

    pairs = ((up_ref, up_out), (dn_ref, dn_out))

    def recv_desc(i, slot):
        dst = pairs[i][1]
        return pltpu.make_async_remote_copy(
            src_ref=dst.at[c, slot],
            dst_ref=dst.at[c, slot],
            send_sem=send_sem.at[i, 0],
            recv_sem=recv_sem.at[i, slot],
            device_id=(slot, mc, c),
            device_id_type=MESH_ID,
        )

    locals_ = []
    sends = []
    for i, (src, dst) in enumerate(pairs):
        cp = pltpu.make_async_copy(src, dst.at[c, me], local_sem.at[i])
        cp.start()
        locals_.append(cp)
        for j, t in enumerate([partner] + [xo + zl for xo in xs]):
            cp = pltpu.make_async_remote_copy(
                src_ref=src,
                dst_ref=dst.at[c, me],
                send_sem=send_sem.at[i, j],
                recv_sem=recv_sem.at[i, me],
                device_id=(t, mc, c),
                device_id_type=MESH_ID,
            )
            cp.start()
            sends.append(cp)
    for i, (src, dst) in enumerate(pairs):
        recv_desc(i, partner).wait_recv()
        for j, xo in enumerate(xs):
            cp = pltpu.make_async_remote_copy(
                src_ref=dst.at[c, partner],
                dst_ref=dst.at[c, partner],
                send_sem=send_sem.at[i, n_x + j],
                recv_sem=recv_sem.at[i, partner],
                device_id=(xo + zl, mc, c),
                device_id_type=MESH_ID,
            )
            cp.start()
            sends.append(cp)

    forwards = []
    for i, (src, dst) in enumerate(pairs):
        order = [me, partner] + [xo + zl for xo in xs] + [xo + 1 - zl for xo in xs]
        for slot in order:
            if slot is me:
                locals_[i].wait()
            elif slot is not partner:
                recv_desc(i, slot).wait_recv()
            fw = pltpu.make_async_remote_copy(
                src_ref=dst.at[c, slot],
                dst_ref=dst.at[c, slot],
                send_sem=fwd_send.at[i, slot],
                recv_sem=fwd_recv.at[i, slot],
                device_id=(me, mc, other),
                device_id_type=MESH_ID,
            )
            fw.start()
            forwards.append(fw)

    for cp in sends:
        cp.wait_send()
    for i, (src, dst) in enumerate(pairs):
        for slot in range(n_rep):
            pltpu.make_async_remote_copy(
                src_ref=dst.at[other, slot],
                dst_ref=dst.at[other, slot],
                send_sem=fwd_send.at[i, slot],
                recv_sem=fwd_recv.at[i, slot],
                device_id=(me, mc, other),
                device_id_type=MESH_ID,
            ).wait_recv()
    for fw in forwards:
        fw.wait_send()


def handover(up_blk, dn_blk, n_rep):
    units, width = up_blk.shape
    shape = jax.ShapeDtypeStruct((2, n_rep, units, width), up_blk.dtype)
    return pl.pallas_call(
        handover_kernel,
        out_shape=(shape, shape),
        in_specs=[pl.BlockSpec(memory_space=pl.ANY)] * 2,
        out_specs=(pl.BlockSpec(memory_space=pl.ANY),) * 2,
        scratch_shapes=[
            pltpu.SemaphoreType.DMA((2, n_rep)),
            pltpu.SemaphoreType.DMA((2, n_rep)),
            pltpu.SemaphoreType.DMA((2, n_rep)),
            pltpu.SemaphoreType.DMA((2, n_rep)),
            pltpu.SemaphoreType.DMA((2,)),
        ],
        compiler_params=pltpu.CompilerParams(collective_id=0, has_side_effects=True),
    )(up_blk, dn_blk)


def local(tokens, prompt_ids, modulation, trainer_up, trainer_down):
    as_float = tokens[0].astype(jnp.float32)
    average = jnp.mean(as_float, axis=-1, keepdims=True)
    centred = as_float - average
    variance = jnp.mean(centred * centred, axis=-1, keepdims=True)
    normed = centred / jnp.sqrt(variance + 1e-06)
    prompts_here = modulation.shape[1]
    onehot = (prompt_ids[0][:, None] == jnp.arange(prompts_here, dtype=jnp.int32)[None, :]).astype(
        jnp.float32
    )
    chosen = jnp.einsum("tp,pkd->tkd", onehot, modulation[0], precision=lax.Precision.HIGHEST)
    shift = chosen[:, 0]
    scale = chosen[:, 1]
    gate = chosen[:, 2]
    xin = (normed * (1.0 + scale) + shift).astype(jnp.bfloat16)

    n_mp = lax.psum(1, MP)
    n_rep = lax.psum(1, "rep")
    rows, cols = trainer_up.shape
    piece = cols // n_mp
    both = jnp.stack([trainer_up.astype(jnp.bfloat16).T, trainer_down.astype(jnp.bfloat16)])
    padded = -(-piece // 16) * 16
    both = jnp.pad(both.reshape(2, n_mp, piece, rows), ((0, 0), (0, 0), (0, padded - piece), (0, 0)))
    both = exchange(both.transpose(1, 0, 2, 3))
    xin, both = lax.optimization_barrier((xin, both))
    x_all = lax.all_gather(xin, "mc", axis=0, tiled=True)
    both = both.transpose(1, 2, 0, 3).reshape(2, padded, n_mp * rows)
    up_all, dn_all = handover(both[0], both[1], n_rep)
    units = 2 * n_rep * padded
    w_up_t = up_all.reshape(units, n_mp * rows)
    w_down = dn_all.reshape(units, n_mp * rows)

    hidden = jax.nn.gelu(
        lax.dot_general(x_all, w_up_t, (((1,), (1,)), ((), ())), preferred_element_type=jnp.float32),
        approximate=True,
    ).astype(jnp.bfloat16)
    mlp = lax.psum_scatter(
        jnp.dot(hidden, w_down, preferred_element_type=jnp.float32).astype(jnp.bfloat16),
        "mc",
        scatter_dimension=0,
        tiled=True,
    ).astype(jnp.float32)
    result = as_float + gate * mlp
    return result.astype(jnp.bfloat16)[None]


def solution(mesh):
    n_rep, n_mp = mesh.devices.shape
    chips = Mesh(mesh.devices.reshape(n_rep, n_mp // 2, 2), ("rep", "mc", "core"))
    in_specs = (
        P("rep", MP, None),
        P("rep", MP),
        P("rep", None, None, None),
        P(MP, "rep"),
        P("rep", MP),
    )
    out_specs = P("rep", MP, None)
    return jax.shard_map(local, mesh=chips, in_specs=in_specs, out_specs=out_specs, check_vma=False)
```

```python
import functools

import jax
import jax.numpy as jnp
from jax import lax
from jax.experimental import pallas as pl
from jax.experimental.pallas import tpu as pltpu
from jax.sharding import Mesh, PartitionSpec as P

MP = ("mc", "core")
MESH_ID = pl.DeviceIdType.MESH


def exchange_kernel(src, dst, send_sem, recv_sem, local_sem):
    n = src.shape[0]
    me = lax.axis_index("mc") * 2 + lax.axis_index("core")
    r = lax.axis_index("rep")

    def dev(i):
        return (r, lax.div(i, 2), lax.rem(i, 2))

    barrier = pltpu.get_barrier_semaphore()
    for k in range(1, n):
        pl.semaphore_signal(barrier, 1, device_id=dev(lax.rem(me + k, n)), device_id_type=MESH_ID)
    pl.semaphore_wait(barrier, n - 1)
    own = pltpu.make_async_copy(src.at[me], dst.at[me], local_sem.at[0])
    own.start()
    sends = []
    for k in range(1, n):
        t = lax.rem(me + k, n)
        cp = pltpu.make_async_remote_copy(
            src_ref=src.at[t],
            dst_ref=dst.at[me],
            send_sem=send_sem.at[k],
            recv_sem=recv_sem.at[k],
            device_id=dev(t),
            device_id_type=MESH_ID,
        )
        cp.start()
        sends.append(cp)
    for k in range(1, n):
        s = lax.rem(me + n - k, n)
        pltpu.make_async_remote_copy(
            src_ref=src.at[s],
            dst_ref=dst.at[s],
            send_sem=send_sem.at[k],
            recv_sem=recv_sem.at[k],
            device_id=dev(s),
            device_id_type=MESH_ID,
        ).wait_recv()
    for cp in sends:
        cp.wait_send()
    own.wait()


def exchange(pieces):
    n = pieces.shape[0]
    return pl.pallas_call(
        exchange_kernel,
        out_shape=jax.ShapeDtypeStruct(pieces.shape, pieces.dtype),
        in_specs=[pl.BlockSpec(memory_space=pl.ANY)],
        out_specs=pl.BlockSpec(memory_space=pl.ANY),
        scratch_shapes=[
            pltpu.SemaphoreType.DMA((n,)),
            pltpu.SemaphoreType.DMA((n,)),
            pltpu.SemaphoreType.DMA((1,)),
        ],
        compiler_params=pltpu.CompilerParams(collective_id=1, has_side_effects=True),
    )(pieces)


def handover_kernel(up_ref, dn_ref, up_out, dn_out, send_sem, recv_sem, fwd_send, fwd_recv, local_sem):
    n_rep = up_out.shape[1]
    n_x = n_rep // 2
    me = lax.axis_index("rep")
    mc = lax.axis_index("mc")
    c = lax.axis_index("core")
    other = 1 - c
    x = lax.div(me, 2)
    zl = lax.rem(me, 2)
    partner = me + 1 - 2 * zl
    xs = [lax.rem(x + d, n_x) * 2 for d in range(1, n_x)]

    barrier = pltpu.get_barrier_semaphore()
    for t in [partner] + [xo + zl for xo in xs]:
        pl.semaphore_signal(barrier, 1, device_id=(t, mc, c), device_id_type=MESH_ID)
    pl.semaphore_signal(barrier, 1, device_id=(me, mc, other), device_id_type=MESH_ID)
    pl.semaphore_wait(barrier, n_x + 1)

    pairs = ((up_ref, up_out), (dn_ref, dn_out))

    def recv_desc(i, slot):
        dst = pairs[i][1]
        return pltpu.make_async_remote_copy(
            src_ref=dst.at[c, slot],
            dst_ref=dst.at[c, slot],
            send_sem=send_sem.at[i, 0],
            recv_sem=recv_sem.at[i, slot],
            device_id=(slot, mc, c),
            device_id_type=MESH_ID,
        )

    locals_ = []
    sends = []
    for i, (src, dst) in enumerate(pairs):
        cp = pltpu.make_async_copy(src, dst.at[c, me], local_sem.at[i])
        cp.start()
        locals_.append(cp)
        for j, t in enumerate([partner] + [xo + zl for xo in xs]):
            cp = pltpu.make_async_remote_copy(
                src_ref=src,
                dst_ref=dst.at[c, me],
                send_sem=send_sem.at[i, j],
                recv_sem=recv_sem.at[i, me],
                device_id=(t, mc, c),
                device_id_type=MESH_ID,
            )
            cp.start()
            sends.append(cp)
    for i, (src, dst) in enumerate(pairs):
        recv_desc(i, partner).wait_recv()
        for j, xo in enumerate(xs):
            cp = pltpu.make_async_remote_copy(
                src_ref=dst.at[c, partner],
                dst_ref=dst.at[c, partner],
                send_sem=send_sem.at[i, n_x + j],
                recv_sem=recv_sem.at[i, partner],
                device_id=(xo + zl, mc, c),
                device_id_type=MESH_ID,
            )
            cp.start()
            sends.append(cp)

    forwards = []
    for i, (src, dst) in enumerate(pairs):
        order = [me, partner] + [xo + zl for xo in xs] + [xo + 1 - zl for xo in xs]
        for slot in order:
            if slot is me:
                locals_[i].wait()
            elif slot is not partner:
                recv_desc(i, slot).wait_recv()
            fw = pltpu.make_async_remote_copy(
                src_ref=dst.at[c, slot],
                dst_ref=dst.at[c, slot],
                send_sem=fwd_send.at[i, slot],
                recv_sem=fwd_recv.at[i, slot],
                device_id=(me, mc, other),
                device_id_type=MESH_ID,
            )
            fw.start()
            forwards.append(fw)

    for cp in sends:
        cp.wait_send()
    for i, (src, dst) in enumerate(pairs):
        for slot in range(n_rep):
            pltpu.make_async_remote_copy(
                src_ref=dst.at[other, slot],
                dst_ref=dst.at[other, slot],
                send_sem=fwd_send.at[i, slot],
                recv_sem=fwd_recv.at[i, slot],
                device_id=(me, mc, other),
                device_id_type=MESH_ID,
            ).wait_recv()
    for fw in forwards:
        fw.wait_send()


def handover(up_blk, dn_blk, n_rep):
    units, width = up_blk.shape
    shape = jax.ShapeDtypeStruct((2, n_rep, units, width), up_blk.dtype)
    return pl.pallas_call(
        handover_kernel,
        out_shape=(shape, shape),
        in_specs=[pl.BlockSpec(memory_space=pl.ANY)] * 2,
        out_specs=(pl.BlockSpec(memory_space=pl.ANY),) * 2,
        scratch_shapes=[
            pltpu.SemaphoreType.DMA((2, n_rep)),
            pltpu.SemaphoreType.DMA((2, n_rep)),
            pltpu.SemaphoreType.DMA((2, n_rep)),
            pltpu.SemaphoreType.DMA((2, n_rep)),
            pltpu.SemaphoreType.DMA((2,)),
        ],
        compiler_params=pltpu.CompilerParams(collective_id=0, has_side_effects=True),
    )(up_blk, dn_blk)


def local(tokens, prompt_ids, modulation, trainer_up, trainer_down):
    as_float = tokens[0].astype(jnp.float32)
    average = jnp.mean(as_float, axis=-1, keepdims=True)
    centred = as_float - average
    variance = jnp.mean(centred * centred, axis=-1, keepdims=True)
    normed = centred / jnp.sqrt(variance + 1e-06)
    prompts_here = modulation.shape[1]
    onehot = (prompt_ids[0][:, None] == jnp.arange(prompts_here, dtype=jnp.int32)[None, :]).astype(
        jnp.float32
    )
    chosen = jnp.einsum("tp,pkd->tkd", onehot, modulation[0], precision=lax.Precision.HIGHEST)
    shift = chosen[:, 0]
    scale = chosen[:, 1]
    gate = chosen[:, 2]
    xin = (normed * (1.0 + scale) + shift).astype(jnp.bfloat16)

    n_mp = lax.psum(1, MP)
    n_rep = lax.psum(1, "rep")
    rows, cols = trainer_up.shape
    piece = cols // n_mp
    both = jnp.stack([trainer_up.astype(jnp.bfloat16).T, trainer_down.astype(jnp.bfloat16)])
    padded = -(-piece // 16) * 16
    both = jnp.pad(both.reshape(2, n_mp, piece, rows), ((0, 0), (0, 0), (0, padded - piece), (0, 0)))
    both = exchange(both.transpose(1, 0, 2, 3))
    both = both.transpose(1, 2, 0, 3).reshape(2, padded, n_mp * rows)
    up_all, dn_all = handover(both[0], both[1], n_rep)
    units = 2 * n_rep * padded
    w_up_t = up_all.reshape(units, n_mp * rows)
    w_down = dn_all.reshape(units, n_mp * rows)

    chunks = 2
    step = xin.shape[0] // chunks
    parts = []
    for h in range(chunks):
        x_all = lax.all_gather(xin[h * step:(h + 1) * step], "mc", axis=0, tiled=True)
        hidden = jax.nn.gelu(
            lax.dot_general(x_all, w_up_t, (((1,), (1,)), ((), ())), preferred_element_type=jnp.float32),
            approximate=True,
        ).astype(jnp.bfloat16)
        parts.append(
            lax.psum_scatter(
                jnp.dot(hidden, w_down, preferred_element_type=jnp.float32).astype(jnp.bfloat16),
                "mc",
                scatter_dimension=0,
                tiled=True,
            )
        )
    mlp = jnp.concatenate(parts, axis=0).astype(jnp.float32)
    result = as_float + gate * mlp
    return result.astype(jnp.bfloat16)[None]


def solution(mesh):
    n_rep, n_mp = mesh.devices.shape
    chips = Mesh(mesh.devices.reshape(n_rep, n_mp // 2, 2), ("rep", "mc", "core"))
    in_specs = (
        P("rep", MP, None),
        P("rep", MP),
        P("rep", None, None, None),
        P(MP, "rep"),
        P("rep", MP),
    )
    out_specs = P("rep", MP, None)
    return jax.shard_map(local, mesh=chips, in_specs=in_specs, out_specs=out_specs, check_vma=False)
```

```python
import functools

import jax
import jax.numpy as jnp
from jax import lax
from jax.experimental import pallas as pl
from jax.experimental.pallas import tpu as pltpu
from jax.sharding import Mesh, PartitionSpec as P

MP = ("zh", "y", "core")
MESH_ID = pl.DeviceIdType.MESH


def exchange_kernel(src, dst, send_sem, recv_sem, local_sem):
    n = src.shape[0]
    me = (lax.axis_index("zh") * 4 + lax.axis_index("y")) * 2 + lax.axis_index("core")
    r = lax.axis_index("rep")

    def dev(i):
        return (r, lax.div(i, 8), lax.rem(lax.div(i, 2), 4), lax.rem(i, 2))

    barrier = pltpu.get_barrier_semaphore()
    for k in range(1, n):
        pl.semaphore_signal(barrier, 1, device_id=dev(lax.rem(me + k, n)), device_id_type=MESH_ID)
    pl.semaphore_wait(barrier, n - 1)
    own = pltpu.make_async_copy(src.at[me], dst.at[me], local_sem.at[0])
    own.start()
    sends = []
    for k in range(1, n):
        t = lax.rem(me + k, n)
        cp = pltpu.make_async_remote_copy(
            src_ref=src.at[t],
            dst_ref=dst.at[me],
            send_sem=send_sem.at[k],
            recv_sem=recv_sem.at[k],
            device_id=dev(t),
            device_id_type=MESH_ID,
        )
        cp.start()
        sends.append(cp)
    for k in range(1, n):
        s = lax.rem(me + n - k, n)
        pltpu.make_async_remote_copy(
            src_ref=src.at[s],
            dst_ref=dst.at[s],
            send_sem=send_sem.at[k],
            recv_sem=recv_sem.at[k],
            device_id=dev(s),
            device_id_type=MESH_ID,
        ).wait_recv()
    for cp in sends:
        cp.wait_send()
    own.wait()


def exchange(pieces):
    n = pieces.shape[0]
    return pl.pallas_call(
        exchange_kernel,
        out_shape=jax.ShapeDtypeStruct(pieces.shape, pieces.dtype),
        in_specs=[pl.BlockSpec(memory_space=pl.ANY)],
        out_specs=pl.BlockSpec(memory_space=pl.ANY),
        scratch_shapes=[
            pltpu.SemaphoreType.DMA((n,)),
            pltpu.SemaphoreType.DMA((n,)),
            pltpu.SemaphoreType.DMA((1,)),
        ],
        compiler_params=pltpu.CompilerParams(collective_id=1, has_side_effects=True),
    )(pieces)


def handover_kernel(up_ref, dn_ref, up_out, dn_out, send_sem, recv_sem, fwd_send, fwd_recv, local_sem):
    n_rep = up_out.shape[1]
    n_x = n_rep // 2
    me = lax.axis_index("rep")
    zh = lax.axis_index("zh")
    yy = lax.axis_index("y")
    c = lax.axis_index("core")
    other = 1 - c
    x = lax.div(me, 2)
    zl = lax.rem(me, 2)
    partner = me + 1 - 2 * zl
    xs = [lax.rem(x + d, n_x) * 2 for d in range(1, n_x)]

    barrier = pltpu.get_barrier_semaphore()
    for t in [partner] + [xo + zl for xo in xs]:
        pl.semaphore_signal(barrier, 1, device_id=(t, zh, yy, c), device_id_type=MESH_ID)
    pl.semaphore_signal(barrier, 1, device_id=(me, zh, yy, other), device_id_type=MESH_ID)
    pl.semaphore_wait(barrier, n_x + 1)

    pairs = ((up_ref, up_out), (dn_ref, dn_out))

    def recv_desc(i, slot):
        dst = pairs[i][1]
        return pltpu.make_async_remote_copy(
            src_ref=dst.at[c, slot],
            dst_ref=dst.at[c, slot],
            send_sem=send_sem.at[i, 0],
            recv_sem=recv_sem.at[i, slot],
            device_id=(slot, zh, yy, c),
            device_id_type=MESH_ID,
        )

    locals_ = []
    sends = []
    for i, (src, dst) in enumerate(pairs):
        cp = pltpu.make_async_copy(src, dst.at[c, me], local_sem.at[i])
        cp.start()
        locals_.append(cp)
        for j, t in enumerate([partner] + [xo + zl for xo in xs]):
            cp = pltpu.make_async_remote_copy(
                src_ref=src,
                dst_ref=dst.at[c, me],
                send_sem=send_sem.at[i, j],
                recv_sem=recv_sem.at[i, me],
                device_id=(t, zh, yy, c),
                device_id_type=MESH_ID,
            )
            cp.start()
            sends.append(cp)
    for i, (src, dst) in enumerate(pairs):
        recv_desc(i, partner).wait_recv()
        for j, xo in enumerate(xs):
            cp = pltpu.make_async_remote_copy(
                src_ref=dst.at[c, partner],
                dst_ref=dst.at[c, partner],
                send_sem=send_sem.at[i, n_x + j],
                recv_sem=recv_sem.at[i, partner],
                device_id=(xo + zl, zh, yy, c),
                device_id_type=MESH_ID,
            )
            cp.start()
            sends.append(cp)

    forwards = []
    for i, (src, dst) in enumerate(pairs):
        order = [me, partner] + [xo + zl for xo in xs] + [xo + 1 - zl for xo in xs]
        for slot in order:
            if slot is me:
                locals_[i].wait()
            elif slot is not partner:
                recv_desc(i, slot).wait_recv()
            fw = pltpu.make_async_remote_copy(
                src_ref=dst.at[c, slot],
                dst_ref=dst.at[c, slot],
                send_sem=fwd_send.at[i, slot],
                recv_sem=fwd_recv.at[i, slot],
                device_id=(me, zh, yy, other),
                device_id_type=MESH_ID,
            )
            fw.start()
            forwards.append(fw)

    for cp in sends:
        cp.wait_send()
    for i, (src, dst) in enumerate(pairs):
        for slot in range(n_rep):
            pltpu.make_async_remote_copy(
                src_ref=dst.at[other, slot],
                dst_ref=dst.at[other, slot],
                send_sem=fwd_send.at[i, slot],
                recv_sem=fwd_recv.at[i, slot],
                device_id=(me, zh, yy, other),
                device_id_type=MESH_ID,
            ).wait_recv()
    for fw in forwards:
        fw.wait_send()


def handover(up_blk, dn_blk, n_rep):
    units, width = up_blk.shape
    shape = jax.ShapeDtypeStruct((2, n_rep, units, width), up_blk.dtype)
    return pl.pallas_call(
        handover_kernel,
        out_shape=(shape, shape),
        in_specs=[pl.BlockSpec(memory_space=pl.ANY)] * 2,
        out_specs=(pl.BlockSpec(memory_space=pl.ANY),) * 2,
        scratch_shapes=[
            pltpu.SemaphoreType.DMA((2, n_rep)),
            pltpu.SemaphoreType.DMA((2, n_rep)),
            pltpu.SemaphoreType.DMA((2, n_rep)),
            pltpu.SemaphoreType.DMA((2, n_rep)),
            pltpu.SemaphoreType.DMA((2,)),
        ],
        compiler_params=pltpu.CompilerParams(collective_id=0, has_side_effects=True),
    )(up_blk, dn_blk)


def local(tokens, prompt_ids, modulation, trainer_up, trainer_down):
    as_float = tokens[0].astype(jnp.float32)
    average = jnp.mean(as_float, axis=-1, keepdims=True)
    centred = as_float - average
    variance = jnp.mean(centred * centred, axis=-1, keepdims=True)
    normed = centred / jnp.sqrt(variance + 1e-06)
    prompts_here = modulation.shape[1]
    onehot = (prompt_ids[0][:, None] == jnp.arange(prompts_here, dtype=jnp.int32)[None, :]).astype(
        jnp.float32
    )
    chosen = jnp.einsum("tp,pkd->tkd", onehot, modulation[0], precision=lax.Precision.HIGHEST)
    shift = chosen[:, 0]
    scale = chosen[:, 1]
    gate = chosen[:, 2]
    xin = (normed * (1.0 + scale) + shift).astype(jnp.bfloat16)

    n_mp = lax.psum(1, MP)
    n_rep = lax.psum(1, "rep")
    rows, cols = trainer_up.shape
    piece = cols // n_mp
    both = jnp.stack([trainer_up.astype(jnp.bfloat16).T, trainer_down.astype(jnp.bfloat16)])
    padded = -(-piece // 16) * 16
    both = jnp.pad(both.reshape(2, n_mp, piece, rows), ((0, 0), (0, 0), (0, padded - piece), (0, 0)))
    both = exchange(both.transpose(1, 0, 2, 3))
    xin, both = lax.optimization_barrier((xin, both))
    x_all = lax.all_gather(lax.all_gather(xin, "zh", axis=0, tiled=True), "y", axis=0, tiled=True)
    both = both.transpose(1, 2, 0, 3).reshape(2, padded, n_mp * rows)
    up_all, dn_all = handover(both[0], both[1], n_rep)
    units = 2 * n_rep * padded
    w_up_t = up_all.reshape(units, n_mp * rows)
    w_down = dn_all.reshape(units, n_mp * rows)

    hidden = jax.nn.gelu(
        lax.dot_general(x_all, w_up_t, (((1,), (1,)), ((), ())), preferred_element_type=jnp.float32),
        approximate=True,
    ).astype(jnp.bfloat16)
    partial = jnp.dot(hidden, w_down, preferred_element_type=jnp.float32).astype(jnp.bfloat16)
    partial = lax.psum_scatter(partial, "y", scatter_dimension=0, tiled=True)
    mlp = lax.psum_scatter(partial, "zh", scatter_dimension=0, tiled=True).astype(jnp.float32)
    result = as_float + gate * mlp
    return result.astype(jnp.bfloat16)[None]


def solution(mesh):
    n_rep, n_mp = mesh.devices.shape
    chips = Mesh(mesh.devices.reshape(n_rep, 4, n_mp // 8, 2), ("rep", "zh", "y", "core"))
    in_specs = (
        P("rep", MP, None),
        P("rep", MP),
        P("rep", None, None, None),
        P(MP, "rep"),
        P("rep", MP),
    )
    out_specs = P("rep", MP, None)
    return jax.shard_map(local, mesh=chips, in_specs=in_specs, out_specs=out_specs, check_vma=False)
```

```python
import functools

import jax
import jax.numpy as jnp
from jax import lax
from jax.experimental import pallas as pl
from jax.experimental.pallas import tpu as pltpu
from jax.sharding import Mesh, PartitionSpec as P

MP = ("mc", "core")
MESH_ID = pl.DeviceIdType.MESH


def exchange_kernel(src, dst, send_sem, recv_sem, local_sem):
    n = src.shape[0]
    me = lax.axis_index("mc") * 2 + lax.axis_index("core")
    r = lax.axis_index("rep")

    def dev(i):
        return (r, lax.div(i, 2), lax.rem(i, 2))

    barrier = pltpu.get_barrier_semaphore()
    for k in range(1, n):
        pl.semaphore_signal(barrier, 1, device_id=dev(lax.rem(me + k, n)), device_id_type=MESH_ID)
    pl.semaphore_wait(barrier, n - 1)
    own = pltpu.make_async_copy(src.at[me], dst.at[me], local_sem.at[0])
    own.start()
    sends = []
    for k in range(1, n):
        t = lax.rem(me + k, n)
        cp = pltpu.make_async_remote_copy(
            src_ref=src.at[t],
            dst_ref=dst.at[me],
            send_sem=send_sem.at[k],
            recv_sem=recv_sem.at[k],
            device_id=dev(t),
            device_id_type=MESH_ID,
        )
        cp.start()
        sends.append(cp)
    for k in range(1, n):
        s = lax.rem(me + n - k, n)
        pltpu.make_async_remote_copy(
            src_ref=src.at[s],
            dst_ref=dst.at[s],
            send_sem=send_sem.at[k],
            recv_sem=recv_sem.at[k],
            device_id=dev(s),
            device_id_type=MESH_ID,
        ).wait_recv()
    for cp in sends:
        cp.wait_send()
    own.wait()


def exchange(pieces):
    n = pieces.shape[0]
    return pl.pallas_call(
        exchange_kernel,
        out_shape=jax.ShapeDtypeStruct(pieces.shape, pieces.dtype),
        in_specs=[pl.BlockSpec(memory_space=pl.ANY)],
        out_specs=pl.BlockSpec(memory_space=pl.ANY),
        scratch_shapes=[
            pltpu.SemaphoreType.DMA((n,)),
            pltpu.SemaphoreType.DMA((n,)),
            pltpu.SemaphoreType.DMA((1,)),
        ],
        compiler_params=pltpu.CompilerParams(collective_id=1, has_side_effects=True),
    )(pieces)


def handover_kernel(up_ref, dn_ref, up_out, dn_out, send_sem, recv_sem, fwd_send, fwd_recv, local_sem):
    n_rep = up_out.shape[1]
    n_x = n_rep // 2
    me = lax.axis_index("rep")
    mc = lax.axis_index("mc")
    c = lax.axis_index("core")
    other = 1 - c
    x = lax.div(me, 2)
    zl = lax.rem(me, 2)
    partner = me + 1 - 2 * zl
    xs = [lax.rem(x + d, n_x) * 2 for d in range(1, n_x)]

    barrier = pltpu.get_barrier_semaphore()
    for t in [partner] + [xo + zl for xo in xs]:
        pl.semaphore_signal(barrier, 1, device_id=(t, mc, c), device_id_type=MESH_ID)
    pl.semaphore_signal(barrier, 1, device_id=(me, mc, other), device_id_type=MESH_ID)
    pl.semaphore_wait(barrier, n_x + 1)

    pairs = ((up_ref, up_out), (dn_ref, dn_out))

    def recv_desc(i, slot):
        dst = pairs[i][1]
        return pltpu.make_async_remote_copy(
            src_ref=dst.at[c, slot],
            dst_ref=dst.at[c, slot],
            send_sem=send_sem.at[i, 0],
            recv_sem=recv_sem.at[i, slot],
            device_id=(slot, mc, c),
            device_id_type=MESH_ID,
        )

    locals_ = []
    sends = []
    for i, (src, dst) in enumerate(pairs):
        cp = pltpu.make_async_copy(src, dst.at[c, me], local_sem.at[i])
        cp.start()
        locals_.append(cp)
        for j, t in enumerate([partner] + [xo + zl for xo in xs]):
            cp = pltpu.make_async_remote_copy(
                src_ref=src,
                dst_ref=dst.at[c, me],
                send_sem=send_sem.at[i, j],
                recv_sem=recv_sem.at[i, me],
                device_id=(t, mc, c),
                device_id_type=MESH_ID,
            )
            cp.start()
            sends.append(cp)
    for i, (src, dst) in enumerate(pairs):
        recv_desc(i, partner).wait_recv()
        for j, xo in enumerate(xs):
            cp = pltpu.make_async_remote_copy(
                src_ref=dst.at[c, partner],
                dst_ref=dst.at[c, partner],
                send_sem=send_sem.at[i, n_x + j],
                recv_sem=recv_sem.at[i, partner],
                device_id=(xo + zl, mc, c),
                device_id_type=MESH_ID,
            )
            cp.start()
            sends.append(cp)

    forwards = []
    for i, (src, dst) in enumerate(pairs):
        order = [me, partner] + [xo + zl for xo in xs] + [xo + 1 - zl for xo in xs]
        for slot in order:
            if slot is me:
                locals_[i].wait()
            elif slot is not partner:
                recv_desc(i, slot).wait_recv()
            fw = pltpu.make_async_remote_copy(
                src_ref=dst.at[c, slot],
                dst_ref=dst.at[c, slot],
                send_sem=fwd_send.at[i, slot],
                recv_sem=fwd_recv.at[i, slot],
                device_id=(me, mc, other),
                device_id_type=MESH_ID,
            )
            fw.start()
            forwards.append(fw)

    for cp in sends:
        cp.wait_send()
    for i, (src, dst) in enumerate(pairs):
        for slot in range(n_rep):
            pltpu.make_async_remote_copy(
                src_ref=dst.at[other, slot],
                dst_ref=dst.at[other, slot],
                send_sem=fwd_send.at[i, slot],
                recv_sem=fwd_recv.at[i, slot],
                device_id=(me, mc, other),
                device_id_type=MESH_ID,
            ).wait_recv()
    for fw in forwards:
        fw.wait_send()


def handover(up_blk, dn_blk, n_rep):
    units, width = up_blk.shape
    shape = jax.ShapeDtypeStruct((2, n_rep, units, width), up_blk.dtype)
    return pl.pallas_call(
        handover_kernel,
        out_shape=(shape, shape),
        in_specs=[pl.BlockSpec(memory_space=pl.ANY)] * 2,
        out_specs=(pl.BlockSpec(memory_space=pl.ANY),) * 2,
        scratch_shapes=[
            pltpu.SemaphoreType.DMA((2, n_rep)),
            pltpu.SemaphoreType.DMA((2, n_rep)),
            pltpu.SemaphoreType.DMA((2, n_rep)),
            pltpu.SemaphoreType.DMA((2, n_rep)),
            pltpu.SemaphoreType.DMA((2,)),
        ],
        compiler_params=pltpu.CompilerParams(collective_id=0, has_side_effects=True),
    )(up_blk, dn_blk)


def local(tokens, prompt_ids, modulation, trainer_up, trainer_down):
    as_float = tokens[0].astype(jnp.float32)
    average = jnp.mean(as_float, axis=-1, keepdims=True)
    centred = as_float - average
    variance = jnp.mean(centred * centred, axis=-1, keepdims=True)
    normed = centred / jnp.sqrt(variance + 1e-06)
    prompts_here = modulation.shape[1]
    onehot = (prompt_ids[0][:, None] == jnp.arange(prompts_here, dtype=jnp.int32)[None, :]).astype(
        jnp.float32
    )
    chosen = jnp.einsum("tp,pkd->tkd", onehot, modulation[0], precision=lax.Precision.HIGHEST)
    shift = chosen[:, 0]
    scale = chosen[:, 1]
    gate = chosen[:, 2]
    xin = (normed * (1.0 + scale) + shift).astype(jnp.bfloat16)
    x_all = lax.all_gather(xin, "mc", axis=0, tiled=True)

    n_mp = lax.psum(1, MP)
    n_rep = lax.psum(1, "rep")
    rows, cols = trainer_up.shape
    piece = cols // n_mp
    both = jnp.stack([trainer_up.astype(jnp.bfloat16).T, trainer_down.astype(jnp.bfloat16)])
    padded = -(-piece // 16) * 16
    both = jnp.pad(both.reshape(2, n_mp, piece, rows), ((0, 0), (0, 0), (0, padded - piece), (0, 0)))
    both = exchange(both.transpose(1, 0, 2, 3))
    both = both.transpose(1, 2, 0, 3).reshape(2, padded, n_mp * rows)
    up_all, dn_all = handover(both[0], both[1], n_rep)
    units = 2 * n_rep * padded
    w_up_t = up_all.reshape(units, n_mp * rows)
    w_down = dn_all.reshape(units, n_mp * rows)

    hidden = jax.nn.gelu(
        lax.dot_general(x_all, w_up_t, (((1,), (1,)), ((), ())), preferred_element_type=jnp.float32),
        approximate=True,
    ).astype(jnp.bfloat16)
    mlp = lax.psum_scatter(
        jnp.dot(hidden, w_down, preferred_element_type=jnp.float32).astype(jnp.bfloat16),
        "mc",
        scatter_dimension=0,
        tiled=True,
    ).astype(jnp.float32)
    result = as_float + gate * mlp
    return result.astype(jnp.bfloat16)[None]


def solution(mesh):
    n_rep, n_mp = mesh.devices.shape
    chips = Mesh(mesh.devices.reshape(n_rep, n_mp // 2, 2), ("rep", "mc", "core"))
    in_specs = (
        P("rep", MP, None),
        P("rep", MP),
        P("rep", None, None, None),
        P(MP, "rep"),
        P("rep", MP),
    )
    out_specs = P("rep", MP, None)
    return jax.shard_map(local, mesh=chips, in_specs=in_specs, out_specs=out_specs, check_vma=False)
```

```python
import functools

import jax
import jax.numpy as jnp
from jax import lax
from jax.experimental import pallas as pl
from jax.experimental.pallas import tpu as pltpu
from jax.sharding import Mesh, PartitionSpec as P

MP = ("mc", "core")
MESH_ID = pl.DeviceIdType.MESH


def exchange_kernel(src, dst, send_sem, recv_sem, local_sem):
    n = src.shape[0]
    me = lax.axis_index("mc") * 2 + lax.axis_index("core")
    r = lax.axis_index("rep")

    def dev(i):
        return (r, lax.div(i, 2), lax.rem(i, 2))

    barrier = pltpu.get_barrier_semaphore()
    for k in range(1, n):
        pl.semaphore_signal(barrier, 1, device_id=dev(lax.rem(me + k, n)), device_id_type=MESH_ID)
    pl.semaphore_wait(barrier, n - 1)
    own = pltpu.make_async_copy(src.at[me], dst.at[me], local_sem.at[0])
    own.start()
    sends = []
    for k in range(1, n):
        t = lax.rem(me + k, n)
        cp = pltpu.make_async_remote_copy(
            src_ref=src.at[t],
            dst_ref=dst.at[me],
            send_sem=send_sem.at[k],
            recv_sem=recv_sem.at[k],
            device_id=dev(t),
            device_id_type=MESH_ID,
        )
        cp.start()
        sends.append(cp)
    for k in range(1, n):
        s = lax.rem(me + n - k, n)
        pltpu.make_async_remote_copy(
            src_ref=src.at[s],
            dst_ref=dst.at[s],
            send_sem=send_sem.at[k],
            recv_sem=recv_sem.at[k],
            device_id=dev(s),
            device_id_type=MESH_ID,
        ).wait_recv()
    for cp in sends:
        cp.wait_send()
    own.wait()


def exchange(pieces):
    n = pieces.shape[0]
    return pl.pallas_call(
        exchange_kernel,
        out_shape=jax.ShapeDtypeStruct(pieces.shape, pieces.dtype),
        in_specs=[pl.BlockSpec(memory_space=pl.ANY)],
        out_specs=pl.BlockSpec(memory_space=pl.ANY),
        scratch_shapes=[
            pltpu.SemaphoreType.DMA((n,)),
            pltpu.SemaphoreType.DMA((n,)),
            pltpu.SemaphoreType.DMA((1,)),
        ],
        compiler_params=pltpu.CompilerParams(collective_id=1, has_side_effects=True),
    )(pieces)


def handover_kernel(up_ref, dn_ref, up_out, dn_out, send_sem, recv_sem, fwd_send, fwd_recv, local_sem):
    n_rep = up_out.shape[1]
    n_x = n_rep // 2
    me = lax.axis_index("rep")
    mc = lax.axis_index("mc")
    c = lax.axis_index("core")
    other = 1 - c
    x = lax.div(me, 2)
    zl = lax.rem(me, 2)
    partner = me + 1 - 2 * zl
    xs = [lax.rem(x + d, n_x) * 2 for d in range(1, n_x)]

    barrier = pltpu.get_barrier_semaphore()
    for t in [partner] + [xo + zl for xo in xs]:
        pl.semaphore_signal(barrier, 1, device_id=(t, mc, c), device_id_type=MESH_ID)
    pl.semaphore_signal(barrier, 1, device_id=(me, mc, other), device_id_type=MESH_ID)
    pl.semaphore_wait(barrier, n_x + 1)

    pairs = ((up_ref, up_out), (dn_ref, dn_out))

    def recv_desc(i, slot):
        dst = pairs[i][1]
        return pltpu.make_async_remote_copy(
            src_ref=dst.at[c, slot],
            dst_ref=dst.at[c, slot],
            send_sem=send_sem.at[i, 0],
            recv_sem=recv_sem.at[i, slot],
            device_id=(slot, mc, c),
            device_id_type=MESH_ID,
        )

    locals_ = []
    sends = []
    for i, (src, dst) in enumerate(pairs):
        cp = pltpu.make_async_copy(src, dst.at[c, me], local_sem.at[i])
        cp.start()
        locals_.append(cp)
        for j, t in enumerate([partner] + [xo + zl for xo in xs]):
            cp = pltpu.make_async_remote_copy(
                src_ref=src,
                dst_ref=dst.at[c, me],
                send_sem=send_sem.at[i, j],
                recv_sem=recv_sem.at[i, me],
                device_id=(t, mc, c),
                device_id_type=MESH_ID,
            )
            cp.start()
            sends.append(cp)
    for i, (src, dst) in enumerate(pairs):
        recv_desc(i, partner).wait_recv()
        for j, xo in enumerate(xs):
            cp = pltpu.make_async_remote_copy(
                src_ref=dst.at[c, partner],
                dst_ref=dst.at[c, partner],
                send_sem=send_sem.at[i, n_x + j],
                recv_sem=recv_sem.at[i, partner],
                device_id=(xo + zl, mc, c),
                device_id_type=MESH_ID,
            )
            cp.start()
            sends.append(cp)

    forwards = []
    for i, (src, dst) in enumerate(pairs):
        order = [me, partner] + [xo + zl for xo in xs] + [xo + 1 - zl for xo in xs]
        for slot in order:
            if slot is me:
                locals_[i].wait()
            elif slot is not partner:
                recv_desc(i, slot).wait_recv()
            fw = pltpu.make_async_remote_copy(
                src_ref=dst.at[c, slot],
                dst_ref=dst.at[c, slot],
                send_sem=fwd_send.at[i, slot],
                recv_sem=fwd_recv.at[i, slot],
                device_id=(me, mc, other),
                device_id_type=MESH_ID,
            )
            fw.start()
            forwards.append(fw)

    for cp in sends:
        cp.wait_send()
    for i, (src, dst) in enumerate(pairs):
        for slot in range(n_rep):
            pltpu.make_async_remote_copy(
                src_ref=dst.at[other, slot],
                dst_ref=dst.at[other, slot],
                send_sem=fwd_send.at[i, slot],
                recv_sem=fwd_recv.at[i, slot],
                device_id=(me, mc, other),
                device_id_type=MESH_ID,
            ).wait_recv()
    for fw in forwards:
        fw.wait_send()


def handover(up_blk, dn_blk, n_rep):
    units, width = up_blk.shape
    shape = jax.ShapeDtypeStruct((2, n_rep, units, width), up_blk.dtype)
    return pl.pallas_call(
        handover_kernel,
        out_shape=(shape, shape),
        in_specs=[pl.BlockSpec(memory_space=pl.ANY)] * 2,
        out_specs=(pl.BlockSpec(memory_space=pl.ANY),) * 2,
        scratch_shapes=[
            pltpu.SemaphoreType.DMA((2, n_rep)),
            pltpu.SemaphoreType.DMA((2, n_rep)),
            pltpu.SemaphoreType.DMA((2, n_rep)),
            pltpu.SemaphoreType.DMA((2, n_rep)),
            pltpu.SemaphoreType.DMA((2,)),
        ],
        compiler_params=pltpu.CompilerParams(collective_id=0, has_side_effects=True),
    )(up_blk, dn_blk)


def local(tokens, prompt_ids, modulation, trainer_up, trainer_down):
    as_float = tokens[0].astype(jnp.float32)
    average = jnp.mean(as_float, axis=-1, keepdims=True)
    centred = as_float - average
    variance = jnp.mean(centred * centred, axis=-1, keepdims=True)
    normed = centred / jnp.sqrt(variance + 1e-06)
    prompts_here = modulation.shape[1]
    onehot = (prompt_ids[0][:, None] == jnp.arange(prompts_here, dtype=jnp.int32)[None, :]).astype(
        jnp.float32
    )
    chosen = jnp.einsum("tp,pkd->tkd", onehot, modulation[0], precision=lax.Precision.HIGHEST)
    shift = chosen[:, 0]
    scale = chosen[:, 1]
    gate = chosen[:, 2]
    xin = (normed * (1.0 + scale) + shift).astype(jnp.bfloat16)

    n_mp = lax.psum(1, MP)
    n_rep = lax.psum(1, "rep")
    rows, cols = trainer_up.shape
    piece = cols // n_mp
    both = jnp.stack([trainer_up.astype(jnp.bfloat16).T, trainer_down.astype(jnp.bfloat16)])
    padded = -(-piece // 16) * 16
    flat = (piece * rows // 120, 120)
    both = exchange(both.reshape(2, n_mp, *flat).transpose(1, 0, 2, 3))
    xin, both = lax.optimization_barrier((xin, both))
    x_all = lax.all_gather(xin, "mc", axis=0, tiled=True)
    both = both.reshape(n_mp, 2, piece, rows).transpose(1, 2, 0, 3)
    both = jnp.pad(both, ((0, 0), (0, padded - piece), (0, 0), (0, 0))).reshape(2, padded, n_mp * rows)
    up_all, dn_all = handover(both[0], both[1], n_rep)
    units = 2 * n_rep * padded
    w_up_t = up_all.reshape(units, n_mp * rows)
    w_down = dn_all.reshape(units, n_mp * rows)

    hidden = jax.nn.gelu(
        lax.dot_general(x_all, w_up_t, (((1,), (1,)), ((), ())), preferred_element_type=jnp.float32),
        approximate=True,
    ).astype(jnp.bfloat16)
    mlp = lax.psum_scatter(
        jnp.dot(hidden, w_down, preferred_element_type=jnp.float32).astype(jnp.bfloat16),
        "mc",
        scatter_dimension=0,
        tiled=True,
    ).astype(jnp.float32)
    result = as_float + gate * mlp
    return result.astype(jnp.bfloat16)[None]


def solution(mesh):
    n_rep, n_mp = mesh.devices.shape
    chips = Mesh(mesh.devices.reshape(n_rep, n_mp // 2, 2), ("rep", "mc", "core"))
    in_specs = (
        P("rep", MP, None),
        P("rep", MP),
        P("rep", None, None, None),
        P(MP, "rep"),
        P("rep", MP),
    )
    out_specs = P("rep", MP, None)
    return jax.shard_map(local, mesh=chips, in_specs=in_specs, out_specs=out_specs, check_vma=False)
```

```python
import functools

import jax
import jax.numpy as jnp
from jax import lax
from jax.experimental import pallas as pl
from jax.experimental.pallas import tpu as pltpu
from jax.sharding import Mesh, PartitionSpec as P

MP = ("mc", "core")
MESH_ID = pl.DeviceIdType.MESH


def exchange_kernel(src, dst, send_sem, recv_sem, local_sem):
    n = src.shape[0]
    me = lax.axis_index("mc") * 2 + lax.axis_index("core")
    r = lax.axis_index("rep")

    def dev(i):
        return (r, lax.div(i, 2), lax.rem(i, 2))

    barrier = pltpu.get_barrier_semaphore()
    for k in range(1, n):
        pl.semaphore_signal(barrier, 1, device_id=dev(lax.rem(me + k, n)), device_id_type=MESH_ID)
    pl.semaphore_wait(barrier, n - 1)
    own = pltpu.make_async_copy(src.at[me], dst.at[me], local_sem.at[0])
    own.start()
    sends = []
    for k in range(1, n):
        t = lax.rem(me + k, n)
        cp = pltpu.make_async_remote_copy(
            src_ref=src.at[t],
            dst_ref=dst.at[me],
            send_sem=send_sem.at[k],
            recv_sem=recv_sem.at[k],
            device_id=dev(t),
            device_id_type=MESH_ID,
        )
        cp.start()
        sends.append(cp)
    for k in range(1, n):
        s = lax.rem(me + n - k, n)
        pltpu.make_async_remote_copy(
            src_ref=src.at[s],
            dst_ref=dst.at[s],
            send_sem=send_sem.at[k],
            recv_sem=recv_sem.at[k],
            device_id=dev(s),
            device_id_type=MESH_ID,
        ).wait_recv()
    for cp in sends:
        cp.wait_send()
    own.wait()


def exchange(pieces):
    n = pieces.shape[0]
    return pl.pallas_call(
        exchange_kernel,
        out_shape=jax.ShapeDtypeStruct(pieces.shape, pieces.dtype),
        in_specs=[pl.BlockSpec(memory_space=pl.ANY)],
        out_specs=pl.BlockSpec(memory_space=pl.ANY),
        scratch_shapes=[
            pltpu.SemaphoreType.DMA((n,)),
            pltpu.SemaphoreType.DMA((n,)),
            pltpu.SemaphoreType.DMA((1,)),
        ],
        compiler_params=pltpu.CompilerParams(collective_id=1, has_side_effects=True),
    )(pieces)


def handover_kernel(up_ref, dn_ref, up_out, dn_out, send_sem, recv_sem, fwd_send, fwd_recv, local_sem):
    n_rep = up_out.shape[1]
    n_x = n_rep // 2
    me = lax.axis_index("rep")
    mc = lax.axis_index("mc")
    c = lax.axis_index("core")
    other = 1 - c
    x = lax.div(me, 2)
    zl = lax.rem(me, 2)
    partner = me + 1 - 2 * zl
    xs = [lax.rem(x + d, n_x) * 2 for d in range(1, n_x)]

    barrier = pltpu.get_barrier_semaphore()
    for t in [partner] + [xo + zl for xo in xs]:
        pl.semaphore_signal(barrier, 1, device_id=(t, mc, c), device_id_type=MESH_ID)
    pl.semaphore_signal(barrier, 1, device_id=(me, mc, other), device_id_type=MESH_ID)
    pl.semaphore_wait(barrier, n_x + 1)

    pairs = ((up_ref, up_out), (dn_ref, dn_out))

    def recv_desc(i, slot):
        dst = pairs[i][1]
        return pltpu.make_async_remote_copy(
            src_ref=dst.at[c, slot],
            dst_ref=dst.at[c, slot],
            send_sem=send_sem.at[i, 0],
            recv_sem=recv_sem.at[i, slot],
            device_id=(slot, mc, c),
            device_id_type=MESH_ID,
        )

    locals_ = []
    sends = []
    for i, (src, dst) in enumerate(pairs):
        cp = pltpu.make_async_copy(src, dst.at[c, me], local_sem.at[i])
        cp.start()
        locals_.append(cp)
        for j, t in enumerate([partner] + [xo + zl for xo in xs]):
            cp = pltpu.make_async_remote_copy(
                src_ref=src,
                dst_ref=dst.at[c, me],
                send_sem=send_sem.at[i, j],
                recv_sem=recv_sem.at[i, me],
                device_id=(t, mc, c),
                device_id_type=MESH_ID,
            )
            cp.start()
            sends.append(cp)
    for i, (src, dst) in enumerate(pairs):
        recv_desc(i, partner).wait_recv()
        for j, xo in enumerate(xs):
            cp = pltpu.make_async_remote_copy(
                src_ref=dst.at[c, partner],
                dst_ref=dst.at[c, partner],
                send_sem=send_sem.at[i, n_x + j],
                recv_sem=recv_sem.at[i, partner],
                device_id=(xo + zl, mc, c),
                device_id_type=MESH_ID,
            )
            cp.start()
            sends.append(cp)

    forwards = []
    for i, (src, dst) in enumerate(pairs):
        order = [me, partner] + [xo + zl for xo in xs] + [xo + 1 - zl for xo in xs]
        for slot in order:
            if slot is me:
                locals_[i].wait()
            elif slot is not partner:
                recv_desc(i, slot).wait_recv()
            fw = pltpu.make_async_remote_copy(
                src_ref=dst.at[c, slot],
                dst_ref=dst.at[c, slot],
                send_sem=fwd_send.at[i, slot],
                recv_sem=fwd_recv.at[i, slot],
                device_id=(me, mc, other),
                device_id_type=MESH_ID,
            )
            fw.start()
            forwards.append(fw)

    for cp in sends:
        cp.wait_send()
    for i, (src, dst) in enumerate(pairs):
        for slot in range(n_rep):
            pltpu.make_async_remote_copy(
                src_ref=dst.at[other, slot],
                dst_ref=dst.at[other, slot],
                send_sem=fwd_send.at[i, slot],
                recv_sem=fwd_recv.at[i, slot],
                device_id=(me, mc, other),
                device_id_type=MESH_ID,
            ).wait_recv()
    for fw in forwards:
        fw.wait_send()


def handover(up_blk, dn_blk, n_rep):
    units, width = up_blk.shape
    shape = jax.ShapeDtypeStruct((2, n_rep, units, width), up_blk.dtype)
    return pl.pallas_call(
        handover_kernel,
        out_shape=(shape, shape),
        in_specs=[pl.BlockSpec(memory_space=pl.ANY)] * 2,
        out_specs=(pl.BlockSpec(memory_space=pl.ANY),) * 2,
        scratch_shapes=[
            pltpu.SemaphoreType.DMA((2, n_rep)),
            pltpu.SemaphoreType.DMA((2, n_rep)),
            pltpu.SemaphoreType.DMA((2, n_rep)),
            pltpu.SemaphoreType.DMA((2, n_rep)),
            pltpu.SemaphoreType.DMA((2,)),
        ],
        compiler_params=pltpu.CompilerParams(collective_id=0, has_side_effects=True),
    )(up_blk, dn_blk)


def local(tokens, prompt_ids, modulation, trainer_up, trainer_down):
    as_float = tokens[0].astype(jnp.float32)
    average = jnp.mean(as_float, axis=-1, keepdims=True)
    centred = as_float - average
    variance = jnp.mean(centred * centred, axis=-1, keepdims=True)
    normed = centred / jnp.sqrt(variance + 1e-06)
    prompts_here = modulation.shape[1]
    onehot = (prompt_ids[0][:, None] == jnp.arange(prompts_here, dtype=jnp.int32)[None, :]).astype(
        jnp.float32
    )
    chosen = jnp.einsum("tp,pkd->tkd", onehot, modulation[0], precision=lax.Precision.HIGHEST)
    shift = chosen[:, 0]
    scale = chosen[:, 1]
    gate = chosen[:, 2]
    xin = (normed * (1.0 + scale) + shift).astype(jnp.bfloat16)
    x_all = lax.all_gather(xin, "mc", axis=0, tiled=True)

    n_mp = lax.psum(1, MP)
    n_rep = lax.psum(1, "rep")
    rows, cols = trainer_up.shape
    piece = cols // n_mp
    both = jnp.stack([trainer_up.astype(jnp.bfloat16).T, trainer_down.astype(jnp.bfloat16)])
    padded = -(-piece // 16) * 16
    flat = (piece * rows // 120, 120)
    both = exchange(both.reshape(2, n_mp, *flat).transpose(1, 0, 2, 3))
    both = both.reshape(n_mp, 2, piece, rows).transpose(1, 2, 0, 3)
    both = jnp.pad(both, ((0, 0), (0, padded - piece), (0, 0), (0, 0))).reshape(2, padded, n_mp * rows)
    up_all, dn_all = handover(both[0], both[1], n_rep)
    units = 2 * n_rep * padded
    w_up_t = up_all.reshape(units, n_mp * rows)
    w_down = dn_all.reshape(units, n_mp * rows)

    hidden = jax.nn.gelu(
        lax.dot_general(x_all, w_up_t, (((1,), (1,)), ((), ())), preferred_element_type=jnp.float32),
        approximate=True,
    ).astype(jnp.bfloat16)
    mlp = lax.psum_scatter(
        jnp.dot(hidden, w_down, preferred_element_type=jnp.float32).astype(jnp.bfloat16),
        "mc",
        scatter_dimension=0,
        tiled=True,
    ).astype(jnp.float32)
    result = as_float + gate * mlp
    return result.astype(jnp.bfloat16)[None]


def solution(mesh):
    n_rep, n_mp = mesh.devices.shape
    chips = Mesh(mesh.devices.reshape(n_rep, n_mp // 2, 2), ("rep", "mc", "core"))
    in_specs = (
        P("rep", MP, None),
        P("rep", MP),
        P("rep", None, None, None),
        P(MP, "rep"),
        P("rep", MP),
    )
    out_specs = P("rep", MP, None)
    return jax.shard_map(local, mesh=chips, in_specs=in_specs, out_specs=out_specs, check_vma=False)
```

```python
import functools

import jax
import jax.numpy as jnp
from jax import lax
from jax.experimental import pallas as pl
from jax.experimental.pallas import tpu as pltpu
from jax.sharding import Mesh, PartitionSpec as P

MP = ("mc", "core")
MESH_ID = pl.DeviceIdType.MESH


def exchange_kernel(src, dst, send_sem, recv_sem, local_sem):
    n = src.shape[0]
    me = lax.axis_index("mc") * 2 + lax.axis_index("core")
    r = lax.axis_index("rep")

    def dev(i):
        return (r, lax.div(i, 2), lax.rem(i, 2))

    barrier = pltpu.get_barrier_semaphore()
    for k in range(1, n):
        pl.semaphore_signal(barrier, 1, device_id=dev(lax.rem(me + k, n)), device_id_type=MESH_ID)
    pl.semaphore_wait(barrier, n - 1)
    own = pltpu.make_async_copy(src.at[me], dst.at[me], local_sem.at[0])
    own.start()
    sends = []
    for k in range(1, n):
        t = lax.rem(me + k, n)
        cp = pltpu.make_async_remote_copy(
            src_ref=src.at[t],
            dst_ref=dst.at[me],
            send_sem=send_sem.at[k],
            recv_sem=recv_sem.at[k],
            device_id=dev(t),
            device_id_type=MESH_ID,
        )
        cp.start()
        sends.append(cp)
    for k in range(1, n):
        s = lax.rem(me + n - k, n)
        pltpu.make_async_remote_copy(
            src_ref=src.at[s],
            dst_ref=dst.at[s],
            send_sem=send_sem.at[k],
            recv_sem=recv_sem.at[k],
            device_id=dev(s),
            device_id_type=MESH_ID,
        ).wait_recv()
    for cp in sends:
        cp.wait_send()
    own.wait()


def exchange(pieces):
    n = pieces.shape[0]
    return pl.pallas_call(
        exchange_kernel,
        out_shape=jax.ShapeDtypeStruct(pieces.shape, pieces.dtype),
        in_specs=[pl.BlockSpec(memory_space=pl.ANY)],
        out_specs=pl.BlockSpec(memory_space=pl.ANY),
        scratch_shapes=[
            pltpu.SemaphoreType.DMA((n,)),
            pltpu.SemaphoreType.DMA((n,)),
            pltpu.SemaphoreType.DMA((1,)),
        ],
        compiler_params=pltpu.CompilerParams(collective_id=1, has_side_effects=True),
    )(pieces)


def handover_kernel(up_ref, dn_ref, up_out, dn_out, send_sem, recv_sem, fwd_send, fwd_recv, local_sem):
    n_rep = up_out.shape[1]
    n_x = n_rep // 2
    me = lax.axis_index("rep")
    mc = lax.axis_index("mc")
    c = lax.axis_index("core")
    other = 1 - c
    x = lax.div(me, 2)
    zl = lax.rem(me, 2)
    partner = me + 1 - 2 * zl
    xs = [lax.rem(x + d, n_x) * 2 for d in range(1, n_x)]

    barrier = pltpu.get_barrier_semaphore()
    for t in [partner] + [xo + zl for xo in xs]:
        pl.semaphore_signal(barrier, 1, device_id=(t, mc, c), device_id_type=MESH_ID)
    pl.semaphore_signal(barrier, 1, device_id=(me, mc, other), device_id_type=MESH_ID)
    pl.semaphore_wait(barrier, n_x + 1)

    pairs = ((up_ref, up_out), (dn_ref, dn_out))

    def recv_desc(i, slot):
        dst = pairs[i][1]
        return pltpu.make_async_remote_copy(
            src_ref=dst.at[c, slot],
            dst_ref=dst.at[c, slot],
            send_sem=send_sem.at[i, 0],
            recv_sem=recv_sem.at[i, slot],
            device_id=(slot, mc, c),
            device_id_type=MESH_ID,
        )

    locals_ = []
    sends = []
    for i, (src, dst) in enumerate(pairs):
        cp = pltpu.make_async_copy(src, dst.at[c, me], local_sem.at[i])
        cp.start()
        locals_.append(cp)
        for j, t in enumerate([partner] + [xo + zl for xo in xs]):
            cp = pltpu.make_async_remote_copy(
                src_ref=src,
                dst_ref=dst.at[c, me],
                send_sem=send_sem.at[i, j],
                recv_sem=recv_sem.at[i, me],
                device_id=(t, mc, c),
                device_id_type=MESH_ID,
            )
            cp.start()
            sends.append(cp)
    for i, (src, dst) in enumerate(pairs):
        recv_desc(i, partner).wait_recv()
        for j, xo in enumerate(xs):
            cp = pltpu.make_async_remote_copy(
                src_ref=dst.at[c, partner],
                dst_ref=dst.at[c, partner],
                send_sem=send_sem.at[i, n_x + j],
                recv_sem=recv_sem.at[i, partner],
                device_id=(xo + zl, mc, c),
                device_id_type=MESH_ID,
            )
            cp.start()
            sends.append(cp)

    forwards = []
    for i, (src, dst) in enumerate(pairs):
        order = [me, partner] + [xo + zl for xo in xs] + [xo + 1 - zl for xo in xs]
        for slot in order:
            if slot is me:
                locals_[i].wait()
            elif slot is not partner:
                recv_desc(i, slot).wait_recv()
            fw = pltpu.make_async_remote_copy(
                src_ref=dst.at[c, slot],
                dst_ref=dst.at[c, slot],
                send_sem=fwd_send.at[i, slot],
                recv_sem=fwd_recv.at[i, slot],
                device_id=(me, mc, other),
                device_id_type=MESH_ID,
            )
            fw.start()
            forwards.append(fw)

    for cp in sends:
        cp.wait_send()
    for i, (src, dst) in enumerate(pairs):
        for slot in range(n_rep):
            pltpu.make_async_remote_copy(
                src_ref=dst.at[other, slot],
                dst_ref=dst.at[other, slot],
                send_sem=fwd_send.at[i, slot],
                recv_sem=fwd_recv.at[i, slot],
                device_id=(me, mc, other),
                device_id_type=MESH_ID,
            ).wait_recv()
    for fw in forwards:
        fw.wait_send()


def handover(up_blk, dn_blk, n_rep):
    units, width = up_blk.shape
    shape = jax.ShapeDtypeStruct((2, n_rep, units, width), up_blk.dtype)
    return pl.pallas_call(
        handover_kernel,
        out_shape=(shape, shape),
        in_specs=[pl.BlockSpec(memory_space=pl.ANY)] * 2,
        out_specs=(pl.BlockSpec(memory_space=pl.ANY),) * 2,
        scratch_shapes=[
            pltpu.SemaphoreType.DMA((2, n_rep)),
            pltpu.SemaphoreType.DMA((2, n_rep)),
            pltpu.SemaphoreType.DMA((2, n_rep)),
            pltpu.SemaphoreType.DMA((2, n_rep)),
            pltpu.SemaphoreType.DMA((2,)),
        ],
        compiler_params=pltpu.CompilerParams(collective_id=0, has_side_effects=True),
    )(up_blk, dn_blk)


def local(tokens, prompt_ids, modulation, trainer_up, trainer_down):
    as_float = tokens[0].astype(jnp.float32)
    average = jnp.mean(as_float, axis=-1, keepdims=True)
    centred = as_float - average
    variance = jnp.mean(centred * centred, axis=-1, keepdims=True)
    normed = centred / jnp.sqrt(variance + 1e-06)
    prompts_here = modulation.shape[1]
    onehot = (prompt_ids[0][:, None] == jnp.arange(prompts_here, dtype=jnp.int32)[None, :]).astype(
        jnp.float32
    )
    chosen = jnp.einsum("tp,pkd->tkd", onehot, modulation[0], precision=lax.Precision.HIGHEST)
    shift = chosen[:, 0]
    scale = chosen[:, 1]
    gate = chosen[:, 2]
    xin = (normed * (1.0 + scale) + shift).astype(jnp.bfloat16)

    n_mp = lax.psum(1, MP)
    n_rep = lax.psum(1, "rep")
    rows, cols = trainer_up.shape
    piece = cols // n_mp
    both = jnp.stack([trainer_up.astype(jnp.bfloat16).T, trainer_down.astype(jnp.bfloat16)])
    padded = -(-piece // 16) * 16
    flat = (piece * rows // 120, 120)
    xin, both = lax.optimization_barrier((xin, both.reshape(2, n_mp, *flat).transpose(1, 0, 2, 3)))
    both = exchange(both)
    xin, both = lax.optimization_barrier((xin, both))
    x_all = lax.all_gather(xin, "mc", axis=0, tiled=True)
    both = both.reshape(n_mp, 2, piece, rows).transpose(1, 2, 0, 3)
    both = jnp.pad(both, ((0, 0), (0, padded - piece), (0, 0), (0, 0))).reshape(2, padded, n_mp * rows)
    up_all, dn_all = handover(both[0], both[1], n_rep)
    units = 2 * n_rep * padded
    w_up_t = up_all.reshape(units, n_mp * rows)
    w_down = dn_all.reshape(units, n_mp * rows)

    hidden = jax.nn.gelu(
        lax.dot_general(x_all, w_up_t, (((1,), (1,)), ((), ())), preferred_element_type=jnp.float32),
        approximate=True,
    ).astype(jnp.bfloat16)
    mlp = lax.psum_scatter(
        jnp.dot(hidden, w_down, preferred_element_type=jnp.float32).astype(jnp.bfloat16),
        "mc",
        scatter_dimension=0,
        tiled=True,
    ).astype(jnp.float32)
    result = as_float + gate * mlp
    return result.astype(jnp.bfloat16)[None]


def solution(mesh):
    n_rep, n_mp = mesh.devices.shape
    chips = Mesh(mesh.devices.reshape(n_rep, n_mp // 2, 2), ("rep", "mc", "core"))
    in_specs = (
        P("rep", MP, None),
        P("rep", MP),
        P("rep", None, None, None),
        P(MP, "rep"),
        P("rep", MP),
    )
    out_specs = P("rep", MP, None)
    return jax.shard_map(local, mesh=chips, in_specs=in_specs, out_specs=out_specs, check_vma=False)
```

```python
import functools

import jax
import jax.numpy as jnp
from jax import lax
from jax.experimental import pallas as pl
from jax.experimental.pallas import tpu as pltpu
from jax.sharding import Mesh, PartitionSpec as P

MP = ("mc", "core")
MESH_ID = pl.DeviceIdType.MESH


def exchange_kernel(src, dst, send_sem, recv_sem, local_sem):
    n = src.shape[0]
    me = lax.axis_index("mc") * 2 + lax.axis_index("core")
    r = lax.axis_index("rep")

    def dev(i):
        return (r, lax.div(i, 2), lax.rem(i, 2))

    barrier = pltpu.get_barrier_semaphore()
    for k in range(1, n):
        pl.semaphore_signal(barrier, 1, device_id=dev(lax.rem(me + k, n)), device_id_type=MESH_ID)
    pl.semaphore_wait(barrier, n - 1)
    own = pltpu.make_async_copy(src.at[me], dst.at[me], local_sem.at[0])
    own.start()
    sends = []
    for k in range(1, n):
        t = lax.rem(me + k, n)
        cp = pltpu.make_async_remote_copy(
            src_ref=src.at[t],
            dst_ref=dst.at[me],
            send_sem=send_sem.at[k],
            recv_sem=recv_sem.at[k],
            device_id=dev(t),
            device_id_type=MESH_ID,
        )
        cp.start()
        sends.append(cp)
    for k in range(1, n):
        s = lax.rem(me + n - k, n)
        pltpu.make_async_remote_copy(
            src_ref=src.at[s],
            dst_ref=dst.at[s],
            send_sem=send_sem.at[k],
            recv_sem=recv_sem.at[k],
            device_id=dev(s),
            device_id_type=MESH_ID,
        ).wait_recv()
    for cp in sends:
        cp.wait_send()
    own.wait()


def exchange(pieces):
    n = pieces.shape[0]
    return pl.pallas_call(
        exchange_kernel,
        out_shape=jax.ShapeDtypeStruct(pieces.shape, pieces.dtype),
        in_specs=[pl.BlockSpec(memory_space=pl.ANY)],
        out_specs=pl.BlockSpec(memory_space=pl.ANY),
        scratch_shapes=[
            pltpu.SemaphoreType.DMA((n,)),
            pltpu.SemaphoreType.DMA((n,)),
            pltpu.SemaphoreType.DMA((1,)),
        ],
        compiler_params=pltpu.CompilerParams(collective_id=1, has_side_effects=True),
    )(pieces)


def handover_kernel(up_ref, dn_ref, up_out, dn_out, send_sem, recv_sem, fwd_send, fwd_recv, local_sem):
    n_rep = up_out.shape[1]
    n_x = n_rep // 2
    me = lax.axis_index("rep")
    mc = lax.axis_index("mc")
    c = lax.axis_index("core")
    other = 1 - c
    x = lax.div(me, 2)
    zl = lax.rem(me, 2)
    partner = me + 1 - 2 * zl
    xs = [lax.rem(x + d, n_x) * 2 for d in range(1, n_x)]

    barrier = pltpu.get_barrier_semaphore()
    for t in [partner] + [xo + zl for xo in xs]:
        pl.semaphore_signal(barrier, 1, device_id=(t, mc, c), device_id_type=MESH_ID)
    pl.semaphore_signal(barrier, 1, device_id=(me, mc, other), device_id_type=MESH_ID)
    pl.semaphore_wait(barrier, n_x + 1)

    pairs = ((up_ref, up_out), (dn_ref, dn_out))

    def recv_desc(i, slot):
        dst = pairs[i][1]
        return pltpu.make_async_remote_copy(
            src_ref=dst.at[c, slot],
            dst_ref=dst.at[c, slot],
            send_sem=send_sem.at[i, 0],
            recv_sem=recv_sem.at[i, slot],
            device_id=(slot, mc, c),
            device_id_type=MESH_ID,
        )

    locals_ = []
    sends = []
    for i, (src, dst) in enumerate(pairs):
        cp = pltpu.make_async_copy(src, dst.at[c, me], local_sem.at[i])
        cp.start()
        locals_.append(cp)
        for j, t in enumerate([partner] + [xo + zl for xo in xs]):
            cp = pltpu.make_async_remote_copy(
                src_ref=src,
                dst_ref=dst.at[c, me],
                send_sem=send_sem.at[i, j],
                recv_sem=recv_sem.at[i, me],
                device_id=(t, mc, c),
                device_id_type=MESH_ID,
            )
            cp.start()
            sends.append(cp)
    for i, (src, dst) in enumerate(pairs):
        recv_desc(i, partner).wait_recv()
        for j, xo in enumerate(xs):
            cp = pltpu.make_async_remote_copy(
                src_ref=dst.at[c, partner],
                dst_ref=dst.at[c, partner],
                send_sem=send_sem.at[i, n_x + j],
                recv_sem=recv_sem.at[i, partner],
                device_id=(xo + zl, mc, c),
                device_id_type=MESH_ID,
            )
            cp.start()
            sends.append(cp)

    forwards = []
    for i, (src, dst) in enumerate(pairs):
        order = [me, partner] + [xo + zl for xo in xs] + [xo + 1 - zl for xo in xs]
        for slot in order:
            if slot is me:
                locals_[i].wait()
            elif slot is not partner:
                recv_desc(i, slot).wait_recv()
            fw = pltpu.make_async_remote_copy(
                src_ref=dst.at[c, slot],
                dst_ref=dst.at[c, slot],
                send_sem=fwd_send.at[i, slot],
                recv_sem=fwd_recv.at[i, slot],
                device_id=(me, mc, other),
                device_id_type=MESH_ID,
            )
            fw.start()
            forwards.append(fw)

    for cp in sends:
        cp.wait_send()
    for i, (src, dst) in enumerate(pairs):
        for slot in range(n_rep):
            pltpu.make_async_remote_copy(
                src_ref=dst.at[other, slot],
                dst_ref=dst.at[other, slot],
                send_sem=fwd_send.at[i, slot],
                recv_sem=fwd_recv.at[i, slot],
                device_id=(me, mc, other),
                device_id_type=MESH_ID,
            ).wait_recv()
    for fw in forwards:
        fw.wait_send()


def handover(up_blk, dn_blk, n_rep):
    units, width = up_blk.shape
    shape = jax.ShapeDtypeStruct((2, n_rep, units, width), up_blk.dtype)
    return pl.pallas_call(
        handover_kernel,
        out_shape=(shape, shape),
        in_specs=[pl.BlockSpec(memory_space=pl.ANY)] * 2,
        out_specs=(pl.BlockSpec(memory_space=pl.ANY),) * 2,
        scratch_shapes=[
            pltpu.SemaphoreType.DMA((2, n_rep)),
            pltpu.SemaphoreType.DMA((2, n_rep)),
            pltpu.SemaphoreType.DMA((2, n_rep)),
            pltpu.SemaphoreType.DMA((2, n_rep)),
            pltpu.SemaphoreType.DMA((2,)),
        ],
        compiler_params=pltpu.CompilerParams(collective_id=0, has_side_effects=True),
    )(up_blk, dn_blk)


def local(tokens, prompt_ids, modulation, trainer_up, trainer_down):
    as_float = tokens[0].astype(jnp.float32)
    average = jnp.mean(as_float, axis=-1, keepdims=True)
    centred = as_float - average
    variance = jnp.mean(centred * centred, axis=-1, keepdims=True)
    normed = centred / jnp.sqrt(variance + 1e-06)
    prompts_here = modulation.shape[1]
    onehot = (prompt_ids[0][:, None] == jnp.arange(prompts_here, dtype=jnp.int32)[None, :]).astype(
        jnp.float32
    )
    chosen = jnp.einsum("tp,pkd->tkd", onehot, modulation[0], precision=lax.Precision.HIGHEST)
    shift = chosen[:, 0]
    scale = chosen[:, 1]
    gate = chosen[:, 2]
    xin = (normed * (1.0 + scale) + shift).astype(jnp.bfloat16)

    n_mp = lax.psum(1, MP)
    n_rep = lax.psum(1, "rep")
    rows, cols = trainer_up.shape
    piece = cols // n_mp
    both = jnp.stack([trainer_up.astype(jnp.bfloat16).T, trainer_down.astype(jnp.bfloat16)])
    flat = (piece * rows // 120, 120)
    both = exchange(both.reshape(2, n_mp, *flat).transpose(1, 0, 2, 3))
    xin, both = lax.optimization_barrier((xin, both))
    x_all = lax.all_gather(xin, "mc", axis=0, tiled=True)
    both = both.reshape(n_mp, 2, piece, rows).transpose(1, 2, 0, 3)
    both = both.reshape(2, piece, n_mp * rows)
    up_all, dn_all = handover(both[0], both[1], n_rep)
    units = 2 * n_rep * piece
    w_up_t = up_all.reshape(units, n_mp * rows)
    w_down = dn_all.reshape(units, n_mp * rows)

    hidden = jax.nn.gelu(
        lax.dot_general(x_all, w_up_t, (((1,), (1,)), ((), ())), preferred_element_type=jnp.float32),
        approximate=True,
    ).astype(jnp.bfloat16)
    mlp = lax.psum_scatter(
        jnp.dot(hidden, w_down, preferred_element_type=jnp.float32).astype(jnp.bfloat16),
        "mc",
        scatter_dimension=0,
        tiled=True,
    ).astype(jnp.float32)
    result = as_float + gate * mlp
    return result.astype(jnp.bfloat16)[None]


def solution(mesh):
    n_rep, n_mp = mesh.devices.shape
    chips = Mesh(mesh.devices.reshape(n_rep, n_mp // 2, 2), ("rep", "mc", "core"))
    in_specs = (
        P("rep", MP, None),
        P("rep", MP),
        P("rep", None, None, None),
        P(MP, "rep"),
        P("rep", MP),
    )
    out_specs = P("rep", MP, None)
    return jax.shard_map(local, mesh=chips, in_specs=in_specs, out_specs=out_specs, check_vma=False)
```

```python
import functools

import jax
import jax.numpy as jnp
from jax import lax
from jax.experimental import pallas as pl
from jax.experimental.pallas import tpu as pltpu
from jax.sharding import Mesh, PartitionSpec as P

MP = ("mc", "core")
MESH_ID = pl.DeviceIdType.MESH


def exchange_kernel(up_src, dn_src, up_dst, dn_dst, send_sem, recv_sem, local_sem):
    n = up_src.shape[0]
    me = lax.axis_index("mc") * 2 + lax.axis_index("core")
    r = lax.axis_index("rep")

    def dev(i):
        return (r, lax.div(i, 2), lax.rem(i, 2))

    barrier = pltpu.get_barrier_semaphore()
    for k in range(1, n):
        pl.semaphore_signal(barrier, 1, device_id=dev(lax.rem(me + k, n)), device_id_type=MESH_ID)
    pl.semaphore_wait(barrier, n - 1)
    pairs = ((up_src, up_dst), (dn_src, dn_dst))
    owns = []
    sends = []
    for i, (src, dst) in enumerate(pairs):
        own = pltpu.make_async_copy(src.at[me], dst.at[me], local_sem.at[i])
        own.start()
        owns.append(own)
    for k in range(1, n):
        t = lax.rem(me + k, n)
        for i, (src, dst) in enumerate(pairs):
            cp = pltpu.make_async_remote_copy(
                src_ref=src.at[t],
                dst_ref=dst.at[me],
                send_sem=send_sem.at[i, k],
                recv_sem=recv_sem.at[i, k],
                device_id=dev(t),
                device_id_type=MESH_ID,
            )
            cp.start()
            sends.append(cp)
    for k in range(1, n):
        s = lax.rem(me + n - k, n)
        for i, (src, dst) in enumerate(pairs):
            pltpu.make_async_remote_copy(
                src_ref=src.at[s],
                dst_ref=dst.at[s],
                send_sem=send_sem.at[i, k],
                recv_sem=recv_sem.at[i, k],
                device_id=dev(s),
                device_id_type=MESH_ID,
            ).wait_recv()
    for cp in sends:
        cp.wait_send()
    for own in owns:
        own.wait()


def exchange(up_pieces, dn_pieces):
    n = up_pieces.shape[0]
    shape = jax.ShapeDtypeStruct(up_pieces.shape, up_pieces.dtype)
    return pl.pallas_call(
        exchange_kernel,
        out_shape=(shape, shape),
        in_specs=[pl.BlockSpec(memory_space=pl.ANY)] * 2,
        out_specs=(pl.BlockSpec(memory_space=pl.ANY),) * 2,
        scratch_shapes=[
            pltpu.SemaphoreType.DMA((2, n)),
            pltpu.SemaphoreType.DMA((2, n)),
            pltpu.SemaphoreType.DMA((2,)),
        ],
        compiler_params=pltpu.CompilerParams(collective_id=1, has_side_effects=True),
    )(up_pieces, dn_pieces)


def handover_kernel(up_ref, dn_ref, up_out, dn_out, send_sem, recv_sem, fwd_send, fwd_recv, local_sem):
    n_rep = up_out.shape[1]
    n_x = n_rep // 2
    me = lax.axis_index("rep")
    mc = lax.axis_index("mc")
    c = lax.axis_index("core")
    other = 1 - c
    x = lax.div(me, 2)
    zl = lax.rem(me, 2)
    partner = me + 1 - 2 * zl
    xs = [lax.rem(x + d, n_x) * 2 for d in range(1, n_x)]

    barrier = pltpu.get_barrier_semaphore()
    for t in [partner] + [xo + zl for xo in xs]:
        pl.semaphore_signal(barrier, 1, device_id=(t, mc, c), device_id_type=MESH_ID)
    pl.semaphore_signal(barrier, 1, device_id=(me, mc, other), device_id_type=MESH_ID)
    pl.semaphore_wait(barrier, n_x + 1)

    pairs = ((up_ref, up_out), (dn_ref, dn_out))

    def recv_desc(i, slot):
        dst = pairs[i][1]
        return pltpu.make_async_remote_copy(
            src_ref=dst.at[c, slot],
            dst_ref=dst.at[c, slot],
            send_sem=send_sem.at[i, 0],
            recv_sem=recv_sem.at[i, slot],
            device_id=(slot, mc, c),
            device_id_type=MESH_ID,
        )

    locals_ = []
    sends = []
    for i, (src, dst) in enumerate(pairs):
        cp = pltpu.make_async_copy(src, dst.at[c, me], local_sem.at[i])
        cp.start()
        locals_.append(cp)
        for j, t in enumerate([partner] + [xo + zl for xo in xs]):
            cp = pltpu.make_async_remote_copy(
                src_ref=src,
                dst_ref=dst.at[c, me],
                send_sem=send_sem.at[i, j],
                recv_sem=recv_sem.at[i, me],
                device_id=(t, mc, c),
                device_id_type=MESH_ID,
            )
            cp.start()
            sends.append(cp)
    for i, (src, dst) in enumerate(pairs):
        recv_desc(i, partner).wait_recv()
        for j, xo in enumerate(xs):
            cp = pltpu.make_async_remote_copy(
                src_ref=dst.at[c, partner],
                dst_ref=dst.at[c, partner],
                send_sem=send_sem.at[i, n_x + j],
                recv_sem=recv_sem.at[i, partner],
                device_id=(xo + zl, mc, c),
                device_id_type=MESH_ID,
            )
            cp.start()
            sends.append(cp)

    forwards = []
    for i, (src, dst) in enumerate(pairs):
        order = [me, partner] + [xo + zl for xo in xs] + [xo + 1 - zl for xo in xs]
        for slot in order:
            if slot is me:
                locals_[i].wait()
            elif slot is not partner:
                recv_desc(i, slot).wait_recv()
            fw = pltpu.make_async_remote_copy(
                src_ref=dst.at[c, slot],
                dst_ref=dst.at[c, slot],
                send_sem=fwd_send.at[i, slot],
                recv_sem=fwd_recv.at[i, slot],
                device_id=(me, mc, other),
                device_id_type=MESH_ID,
            )
            fw.start()
            forwards.append(fw)

    for cp in sends:
        cp.wait_send()
    for i, (src, dst) in enumerate(pairs):
        for slot in range(n_rep):
            pltpu.make_async_remote_copy(
                src_ref=dst.at[other, slot],
                dst_ref=dst.at[other, slot],
                send_sem=fwd_send.at[i, slot],
                recv_sem=fwd_recv.at[i, slot],
                device_id=(me, mc, other),
                device_id_type=MESH_ID,
            ).wait_recv()
    for fw in forwards:
        fw.wait_send()


def handover(up_blk, dn_blk, n_rep):
    units, width = up_blk.shape
    shape = jax.ShapeDtypeStruct((2, n_rep, units, width), up_blk.dtype)
    return pl.pallas_call(
        handover_kernel,
        out_shape=(shape, shape),
        in_specs=[pl.BlockSpec(memory_space=pl.ANY)] * 2,
        out_specs=(pl.BlockSpec(memory_space=pl.ANY),) * 2,
        scratch_shapes=[
            pltpu.SemaphoreType.DMA((2, n_rep)),
            pltpu.SemaphoreType.DMA((2, n_rep)),
            pltpu.SemaphoreType.DMA((2, n_rep)),
            pltpu.SemaphoreType.DMA((2, n_rep)),
            pltpu.SemaphoreType.DMA((2,)),
        ],
        compiler_params=pltpu.CompilerParams(collective_id=0, has_side_effects=True),
    )(up_blk, dn_blk)


def local(tokens, prompt_ids, modulation, trainer_up, trainer_down):
    as_float = tokens[0].astype(jnp.float32)
    average = jnp.mean(as_float, axis=-1, keepdims=True)
    centred = as_float - average
    variance = jnp.mean(centred * centred, axis=-1, keepdims=True)
    normed = centred / jnp.sqrt(variance + 1e-06)
    prompts_here = modulation.shape[1]
    onehot = (prompt_ids[0][:, None] == jnp.arange(prompts_here, dtype=jnp.int32)[None, :]).astype(
        jnp.float32
    )
    chosen = jnp.einsum("tp,pkd->tkd", onehot, modulation[0], precision=lax.Precision.HIGHEST)
    shift = chosen[:, 0]
    scale = chosen[:, 1]
    gate = chosen[:, 2]
    xin = (normed * (1.0 + scale) + shift).astype(jnp.bfloat16)

    n_mp = lax.psum(1, MP)
    n_rep = lax.psum(1, "rep")
    rows, cols = trainer_up.shape
    piece = cols // n_mp
    flat = (piece * rows // 120, 120)
    up_p = trainer_up.astype(jnp.bfloat16).reshape(rows, n_mp, piece).transpose(1, 2, 0)
    dn_p = trainer_down.astype(jnp.bfloat16).reshape(n_mp, piece, rows)
    up_p, dn_p = exchange(up_p.reshape(n_mp, *flat), dn_p.reshape(n_mp, *flat))
    xin, up_p, dn_p = lax.optimization_barrier((xin, up_p, dn_p))
    x_all = lax.all_gather(xin, "mc", axis=0, tiled=True)

    def units_by_d(p):
        return p.reshape(n_mp, piece, rows).transpose(1, 0, 2).reshape(piece, n_mp * rows)

    up_all, dn_all = handover(units_by_d(up_p), units_by_d(dn_p), n_rep)
    units = 2 * n_rep * piece
    w_up_t = up_all.reshape(units, n_mp * rows)
    w_down = dn_all.reshape(units, n_mp * rows)

    hidden = jax.nn.gelu(
        lax.dot_general(x_all, w_up_t, (((1,), (1,)), ((), ())), preferred_element_type=jnp.float32),
        approximate=True,
    ).astype(jnp.bfloat16)
    mlp = lax.psum_scatter(
        jnp.dot(hidden, w_down, preferred_element_type=jnp.float32).astype(jnp.bfloat16),
        "mc",
        scatter_dimension=0,
        tiled=True,
    ).astype(jnp.float32)
    result = as_float + gate * mlp
    return result.astype(jnp.bfloat16)[None]


def solution(mesh):
    n_rep, n_mp = mesh.devices.shape
    chips = Mesh(mesh.devices.reshape(n_rep, n_mp // 2, 2), ("rep", "mc", "core"))
    in_specs = (
        P("rep", MP, None),
        P("rep", MP),
        P("rep", None, None, None),
        P(MP, "rep"),
        P("rep", MP),
    )
    out_specs = P("rep", MP, None)
    return jax.shard_map(local, mesh=chips, in_specs=in_specs, out_specs=out_specs, check_vma=False)
```

```python
import functools

import jax
import jax.numpy as jnp
from jax import lax
from jax.experimental import pallas as pl
from jax.experimental.pallas import tpu as pltpu
from jax.sharding import Mesh, PartitionSpec as P

MP = ("mc", "core")
MESH_ID = pl.DeviceIdType.MESH


def exchange_kernel(src, dst, send_sem, recv_sem, local_sem):
    n = src.shape[0]
    me = lax.axis_index("mc") * 2 + lax.axis_index("core")
    r = lax.axis_index("rep")

    def dev(i):
        return (r, lax.div(i, 2), lax.rem(i, 2))

    barrier = pltpu.get_barrier_semaphore()
    for k in range(1, n):
        pl.semaphore_signal(barrier, 1, device_id=dev(lax.rem(me + k, n)), device_id_type=MESH_ID)
    pl.semaphore_wait(barrier, n - 1)
    own = pltpu.make_async_copy(src.at[me], dst.at[me], local_sem.at[0])
    own.start()
    sends = []
    for k in range(1, n):
        t = lax.rem(me + k, n)
        cp = pltpu.make_async_remote_copy(
            src_ref=src.at[t],
            dst_ref=dst.at[me],
            send_sem=send_sem.at[k],
            recv_sem=recv_sem.at[k],
            device_id=dev(t),
            device_id_type=MESH_ID,
        )
        cp.start()
        sends.append(cp)
    for k in range(1, n):
        s = lax.rem(me + n - k, n)
        pltpu.make_async_remote_copy(
            src_ref=src.at[s],
            dst_ref=dst.at[s],
            send_sem=send_sem.at[k],
            recv_sem=recv_sem.at[k],
            device_id=dev(s),
            device_id_type=MESH_ID,
        ).wait_recv()
    for cp in sends:
        cp.wait_send()
    own.wait()


def exchange(pieces):
    n = pieces.shape[0]
    return pl.pallas_call(
        exchange_kernel,
        out_shape=jax.ShapeDtypeStruct(pieces.shape, pieces.dtype),
        in_specs=[pl.BlockSpec(memory_space=pl.ANY)],
        out_specs=pl.BlockSpec(memory_space=pl.ANY),
        scratch_shapes=[
            pltpu.SemaphoreType.DMA((n,)),
            pltpu.SemaphoreType.DMA((n,)),
            pltpu.SemaphoreType.DMA((1,)),
        ],
        compiler_params=pltpu.CompilerParams(collective_id=1, has_side_effects=True),
    )(pieces)


def handover_kernel(up_ref, dn_ref, up_out, dn_out, send_sem, recv_sem, fwd_send, fwd_recv, local_sem):
    n_rep = up_out.shape[1]
    n_x = n_rep // 2
    me = lax.axis_index("rep")
    mc = lax.axis_index("mc")
    c = lax.axis_index("core")
    other = 1 - c
    x = lax.div(me, 2)
    zl = lax.rem(me, 2)
    partner = me + 1 - 2 * zl
    xs = [lax.rem(x + d, n_x) * 2 for d in range(1, n_x)]

    barrier = pltpu.get_barrier_semaphore()
    for t in [partner] + [xo + zl for xo in xs]:
        pl.semaphore_signal(barrier, 1, device_id=(t, mc, c), device_id_type=MESH_ID)
    pl.semaphore_signal(barrier, 1, device_id=(me, mc, other), device_id_type=MESH_ID)
    pl.semaphore_wait(barrier, n_x + 1)

    pairs = ((up_ref, up_out), (dn_ref, dn_out))

    def recv_desc(i, slot):
        dst = pairs[i][1]
        return pltpu.make_async_remote_copy(
            src_ref=dst.at[c, slot],
            dst_ref=dst.at[c, slot],
            send_sem=send_sem.at[i, 0],
            recv_sem=recv_sem.at[i, slot],
            device_id=(slot, mc, c),
            device_id_type=MESH_ID,
        )

    locals_ = []
    sends = []
    for i, (src, dst) in enumerate(pairs):
        cp = pltpu.make_async_copy(src, dst.at[c, me], local_sem.at[i])
        cp.start()
        locals_.append(cp)
        for j, t in enumerate([partner] + [xo + zl for xo in xs]):
            cp = pltpu.make_async_remote_copy(
                src_ref=src,
                dst_ref=dst.at[c, me],
                send_sem=send_sem.at[i, j],
                recv_sem=recv_sem.at[i, me],
                device_id=(t, mc, c),
                device_id_type=MESH_ID,
            )
            cp.start()
            sends.append(cp)
    for i, (src, dst) in enumerate(pairs):
        recv_desc(i, partner).wait_recv()
        for j, xo in enumerate(xs):
            cp = pltpu.make_async_remote_copy(
                src_ref=dst.at[c, partner],
                dst_ref=dst.at[c, partner],
                send_sem=send_sem.at[i, n_x + j],
                recv_sem=recv_sem.at[i, partner],
                device_id=(xo + zl, mc, c),
                device_id_type=MESH_ID,
            )
            cp.start()
            sends.append(cp)

    forwards = []
    for i, (src, dst) in enumerate(pairs):
        order = [me, partner] + [xo + zl for xo in xs] + [xo + 1 - zl for xo in xs]
        for slot in order:
            if slot is me:
                locals_[i].wait()
            elif slot is not partner:
                recv_desc(i, slot).wait_recv()
            fw = pltpu.make_async_remote_copy(
                src_ref=dst.at[c, slot],
                dst_ref=dst.at[c, slot],
                send_sem=fwd_send.at[i, slot],
                recv_sem=fwd_recv.at[i, slot],
                device_id=(me, mc, other),
                device_id_type=MESH_ID,
            )
            fw.start()
            forwards.append(fw)

    for cp in sends:
        cp.wait_send()
    for i, (src, dst) in enumerate(pairs):
        for slot in range(n_rep):
            pltpu.make_async_remote_copy(
                src_ref=dst.at[other, slot],
                dst_ref=dst.at[other, slot],
                send_sem=fwd_send.at[i, slot],
                recv_sem=fwd_recv.at[i, slot],
                device_id=(me, mc, other),
                device_id_type=MESH_ID,
            ).wait_recv()
    for fw in forwards:
        fw.wait_send()


def handover(up_blk, dn_blk, n_rep):
    units, width = up_blk.shape
    shape = jax.ShapeDtypeStruct((2, n_rep, units, width), up_blk.dtype)
    return pl.pallas_call(
        handover_kernel,
        out_shape=(shape, shape),
        in_specs=[pl.BlockSpec(memory_space=pl.ANY)] * 2,
        out_specs=(pl.BlockSpec(memory_space=pl.ANY),) * 2,
        scratch_shapes=[
            pltpu.SemaphoreType.DMA((2, n_rep)),
            pltpu.SemaphoreType.DMA((2, n_rep)),
            pltpu.SemaphoreType.DMA((2, n_rep)),
            pltpu.SemaphoreType.DMA((2, n_rep)),
            pltpu.SemaphoreType.DMA((2,)),
        ],
        compiler_params=pltpu.CompilerParams(collective_id=0, has_side_effects=True),
    )(up_blk, dn_blk)


def local(tokens, prompt_ids, modulation, trainer_up, trainer_down):
    as_float = tokens[0].astype(jnp.float32)
    average = jnp.mean(as_float, axis=-1, keepdims=True)
    centred = as_float - average
    variance = jnp.mean(centred * centred, axis=-1, keepdims=True)
    normed = centred / jnp.sqrt(variance + 1e-06)
    prompts_here = modulation.shape[1]
    onehot = (prompt_ids[0][:, None] == jnp.arange(prompts_here, dtype=jnp.int32)[None, :]).astype(
        jnp.float32
    )
    chosen = jnp.einsum("tp,pkd->tkd", onehot, modulation[0], precision=lax.Precision.HIGHEST)
    shift = chosen[:, 0]
    scale = chosen[:, 1]
    gate = chosen[:, 2]
    xin = (normed * (1.0 + scale) + shift).astype(jnp.bfloat16)

    n_mp = lax.psum(1, MP)
    n_rep = lax.psum(1, "rep")
    rows, cols = trainer_up.shape
    piece = cols // n_mp
    both = jnp.stack([trainer_up.astype(jnp.bfloat16).T, trainer_down.astype(jnp.bfloat16)])
    flat = (2 * piece * rows // 128, 128)
    both = exchange(both.reshape(2, n_mp, piece, rows).transpose(1, 0, 2, 3).reshape(n_mp, *flat))
    xin, both = lax.optimization_barrier((xin, both))
    x_all = lax.all_gather(xin, "mc", axis=0, tiled=True)
    both = both.reshape(n_mp, 2, piece, rows).transpose(1, 2, 0, 3)
    both = both.reshape(2, piece, n_mp * rows)
    up_all, dn_all = handover(both[0], both[1], n_rep)
    units = 2 * n_rep * piece
    w_up_t = up_all.reshape(units, n_mp * rows)
    w_down = dn_all.reshape(units, n_mp * rows)

    hidden = jax.nn.gelu(
        lax.dot_general(x_all, w_up_t, (((1,), (1,)), ((), ())), preferred_element_type=jnp.float32),
        approximate=True,
    ).astype(jnp.bfloat16)
    mlp = lax.psum_scatter(
        jnp.dot(hidden, w_down, preferred_element_type=jnp.float32).astype(jnp.bfloat16),
        "mc",
        scatter_dimension=0,
        tiled=True,
    ).astype(jnp.float32)
    result = as_float + gate * mlp
    return result.astype(jnp.bfloat16)[None]


def solution(mesh):
    n_rep, n_mp = mesh.devices.shape
    chips = Mesh(mesh.devices.reshape(n_rep, n_mp // 2, 2), ("rep", "mc", "core"))
    in_specs = (
        P("rep", MP, None),
        P("rep", MP),
        P("rep", None, None, None),
        P(MP, "rep"),
        P("rep", MP),
    )
    out_specs = P("rep", MP, None)
    return jax.shard_map(local, mesh=chips, in_specs=in_specs, out_specs=out_specs, check_vma=False)
```

```python
import functools

import jax
import jax.numpy as jnp
from jax import lax
from jax.experimental import pallas as pl
from jax.experimental.pallas import tpu as pltpu
from jax.sharding import Mesh, PartitionSpec as P

MP = ("mc", "core")
MESH_ID = pl.DeviceIdType.MESH


def exchange_kernel(src, dst, send_sem, recv_sem, local_sem):
    n = src.shape[0]
    me = lax.axis_index("mc") * 2 + lax.axis_index("core")
    r = lax.axis_index("rep")

    def dev(i):
        return (r, lax.div(i, 2), lax.rem(i, 2))

    barrier = pltpu.get_barrier_semaphore()
    for k in range(1, n):
        pl.semaphore_signal(barrier, 1, device_id=dev(lax.rem(me + k, n)), device_id_type=MESH_ID)
    pl.semaphore_wait(barrier, n - 1)
    own = pltpu.make_async_copy(src.at[me], dst.at[me], local_sem.at[0])
    own.start()
    sends = []
    for k in range(1, n):
        t = lax.rem(me + k, n)
        cp = pltpu.make_async_remote_copy(
            src_ref=src.at[t],
            dst_ref=dst.at[me],
            send_sem=send_sem.at[k],
            recv_sem=recv_sem.at[k],
            device_id=dev(t),
            device_id_type=MESH_ID,
        )
        cp.start()
        sends.append(cp)
    for k in range(1, n):
        s = lax.rem(me + n - k, n)
        pltpu.make_async_remote_copy(
            src_ref=src.at[s],
            dst_ref=dst.at[s],
            send_sem=send_sem.at[k],
            recv_sem=recv_sem.at[k],
            device_id=dev(s),
            device_id_type=MESH_ID,
        ).wait_recv()
    for cp in sends:
        cp.wait_send()
    own.wait()


def exchange(pieces):
    n = pieces.shape[0]
    return pl.pallas_call(
        exchange_kernel,
        out_shape=jax.ShapeDtypeStruct(pieces.shape, pieces.dtype),
        in_specs=[pl.BlockSpec(memory_space=pl.ANY)],
        out_specs=pl.BlockSpec(memory_space=pl.ANY),
        scratch_shapes=[
            pltpu.SemaphoreType.DMA((n,)),
            pltpu.SemaphoreType.DMA((n,)),
            pltpu.SemaphoreType.DMA((1,)),
        ],
        compiler_params=pltpu.CompilerParams(collective_id=1, has_side_effects=True),
    )(pieces)


def handover_kernel(up_ref, dn_ref, up_out, dn_out, send_sem, recv_sem, fwd_send, fwd_recv, local_sem):
    n_rep = up_out.shape[1]
    n_x = n_rep // 2
    me = lax.axis_index("rep")
    mc = lax.axis_index("mc")
    c = lax.axis_index("core")
    other = 1 - c
    x = lax.div(me, 2)
    zl = lax.rem(me, 2)
    partner = me + 1 - 2 * zl
    xs = [lax.rem(x + d, n_x) * 2 for d in range(1, n_x)]

    barrier = pltpu.get_barrier_semaphore()
    for t in [partner] + [xo + zl for xo in xs]:
        pl.semaphore_signal(barrier, 1, device_id=(t, mc, c), device_id_type=MESH_ID)
    pl.semaphore_signal(barrier, 1, device_id=(me, mc, other), device_id_type=MESH_ID)
    pl.semaphore_wait(barrier, n_x + 1)

    pairs = ((up_ref, up_out), (dn_ref, dn_out))

    def recv_desc(i, slot):
        dst = pairs[i][1]
        return pltpu.make_async_remote_copy(
            src_ref=dst.at[c, slot],
            dst_ref=dst.at[c, slot],
            send_sem=send_sem.at[i, 0],
            recv_sem=recv_sem.at[i, slot],
            device_id=(slot, mc, c),
            device_id_type=MESH_ID,
        )

    locals_ = []
    sends = []
    for i, (src, dst) in enumerate(pairs):
        cp = pltpu.make_async_copy(src, dst.at[c, me], local_sem.at[i])
        cp.start()
        locals_.append(cp)
        for j, t in enumerate([partner] + [xo + zl for xo in xs]):
            cp = pltpu.make_async_remote_copy(
                src_ref=src,
                dst_ref=dst.at[c, me],
                send_sem=send_sem.at[i, j],
                recv_sem=recv_sem.at[i, me],
                device_id=(t, mc, c),
                device_id_type=MESH_ID,
            )
            cp.start()
            sends.append(cp)
    for i, (src, dst) in enumerate(pairs):
        recv_desc(i, partner).wait_recv()
        for j, xo in enumerate(xs):
            cp = pltpu.make_async_remote_copy(
                src_ref=dst.at[c, partner],
                dst_ref=dst.at[c, partner],
                send_sem=send_sem.at[i, n_x + j],
                recv_sem=recv_sem.at[i, partner],
                device_id=(xo + zl, mc, c),
                device_id_type=MESH_ID,
            )
            cp.start()
            sends.append(cp)

    forwards = []
    for i, (src, dst) in enumerate(pairs):
        order = [me, partner] + [xo + zl for xo in xs] + [xo + 1 - zl for xo in xs]
        for slot in order:
            if slot is me:
                locals_[i].wait()
            elif slot is not partner:
                recv_desc(i, slot).wait_recv()
            fw = pltpu.make_async_remote_copy(
                src_ref=dst.at[c, slot],
                dst_ref=dst.at[c, slot],
                send_sem=fwd_send.at[i, slot],
                recv_sem=fwd_recv.at[i, slot],
                device_id=(me, mc, other),
                device_id_type=MESH_ID,
            )
            fw.start()
            forwards.append(fw)

    for cp in sends:
        cp.wait_send()
    for i, (src, dst) in enumerate(pairs):
        for slot in range(n_rep):
            pltpu.make_async_remote_copy(
                src_ref=dst.at[other, slot],
                dst_ref=dst.at[other, slot],
                send_sem=fwd_send.at[i, slot],
                recv_sem=fwd_recv.at[i, slot],
                device_id=(me, mc, other),
                device_id_type=MESH_ID,
            ).wait_recv()
    for fw in forwards:
        fw.wait_send()


def handover(up_blk, dn_blk, n_rep):
    units, width = up_blk.shape
    shape = jax.ShapeDtypeStruct((2, n_rep, units, width), up_blk.dtype)
    return pl.pallas_call(
        handover_kernel,
        out_shape=(shape, shape),
        in_specs=[pl.BlockSpec(memory_space=pl.ANY)] * 2,
        out_specs=(pl.BlockSpec(memory_space=pl.ANY),) * 2,
        scratch_shapes=[
            pltpu.SemaphoreType.DMA((2, n_rep)),
            pltpu.SemaphoreType.DMA((2, n_rep)),
            pltpu.SemaphoreType.DMA((2, n_rep)),
            pltpu.SemaphoreType.DMA((2, n_rep)),
            pltpu.SemaphoreType.DMA((2,)),
        ],
        compiler_params=pltpu.CompilerParams(collective_id=0, has_side_effects=True),
    )(up_blk, dn_blk)


def local(tokens, prompt_ids, modulation, trainer_up, trainer_down):
    as_float = tokens[0].astype(jnp.float32)
    average = jnp.mean(as_float, axis=-1, keepdims=True)
    centred = as_float - average
    variance = jnp.mean(centred * centred, axis=-1, keepdims=True)
    normed = centred / jnp.sqrt(variance + 1e-06)
    chosen = jnp.take(modulation[0], prompt_ids[0], axis=0, mode="clip")
    shift = chosen[:, 0]
    scale = chosen[:, 1]
    gate = chosen[:, 2]
    xin = (normed * (1.0 + scale) + shift).astype(jnp.bfloat16)

    n_mp = lax.psum(1, MP)
    n_rep = lax.psum(1, "rep")
    rows, cols = trainer_up.shape
    piece = cols // n_mp
    both = jnp.stack([trainer_up.astype(jnp.bfloat16).T, trainer_down.astype(jnp.bfloat16)])
    flat = (piece * rows // 120, 120)
    both = exchange(both.reshape(2, n_mp, *flat).transpose(1, 0, 2, 3))
    xin, both = lax.optimization_barrier((xin, both))
    x_all = lax.all_gather(xin, "mc", axis=0, tiled=True)
    both = both.reshape(n_mp, 2, piece, rows).transpose(1, 2, 0, 3)
    both = both.reshape(2, piece, n_mp * rows)
    up_all, dn_all = handover(both[0], both[1], n_rep)
    units = 2 * n_rep * piece
    w_up_t = up_all.reshape(units, n_mp * rows)
    w_down = dn_all.reshape(units, n_mp * rows)

    hidden = jax.nn.gelu(
        lax.dot_general(x_all, w_up_t, (((1,), (1,)), ((), ())), preferred_element_type=jnp.float32),
        approximate=True,
    ).astype(jnp.bfloat16)
    mlp = lax.psum_scatter(
        jnp.dot(hidden, w_down, preferred_element_type=jnp.float32).astype(jnp.bfloat16),
        "mc",
        scatter_dimension=0,
        tiled=True,
    ).astype(jnp.float32)
    result = as_float + gate * mlp
    return result.astype(jnp.bfloat16)[None]


def solution(mesh):
    n_rep, n_mp = mesh.devices.shape
    chips = Mesh(mesh.devices.reshape(n_rep, n_mp // 2, 2), ("rep", "mc", "core"))
    in_specs = (
        P("rep", MP, None),
        P("rep", MP),
        P("rep", None, None, None),
        P(MP, "rep"),
        P("rep", MP),
    )
    out_specs = P("rep", MP, None)
    return jax.shard_map(local, mesh=chips, in_specs=in_specs, out_specs=out_specs, check_vma=False)
```

```python
import functools

import jax
import jax.numpy as jnp
from jax import lax
from jax.experimental import pallas as pl
from jax.experimental.pallas import tpu as pltpu
from jax.sharding import Mesh, PartitionSpec as P

MP = ("mc", "core")
MESH_ID = pl.DeviceIdType.MESH


def _offsets(n_zh, n_y):
    ring = lambda d, n: min(d, n - d)
    offs = [(dz, dy, dc) for dz in range(n_zh) for dy in range(n_y) for dc in range(2) if (dz, dy, dc) != (0, 0, 0)]
    return sorted(offs, key=lambda o: -(2 * ring(o[0], n_zh) + ring(o[1], n_y)))


def exchange_kernel(src, dst, send_sem, recv_sem, local_sem):
    n = src.shape[0]
    n_y = 4
    n_zh = n // (2 * n_y)
    mc = lax.axis_index("mc")
    zh = lax.div(mc, n_y)
    yy = lax.rem(mc, n_y)
    c = lax.axis_index("core")
    me = mc * 2 + c
    r = lax.axis_index("rep")
    offsets = _offsets(n_zh, n_y)

    def peer(o, sign):
        z2 = lax.rem(zh + sign * o[0] + n_zh, n_zh)
        y2 = lax.rem(yy + sign * o[1] + n_y, n_y)
        c2 = lax.rem(c + sign * o[2] + 2, 2)
        return (z2 * n_y + y2) * 2 + c2, (r, z2 * n_y + y2, c2)

    barrier = pltpu.get_barrier_semaphore()
    for o in offsets:
        pl.semaphore_signal(barrier, 1, device_id=peer(o, 1)[1], device_id_type=MESH_ID)
    pl.semaphore_wait(barrier, n - 1)
    sends = []
    for j, o in enumerate(offsets):
        t, dev = peer(o, 1)
        cp = pltpu.make_async_remote_copy(
            src_ref=src.at[t],
            dst_ref=dst.at[me],
            send_sem=send_sem.at[j],
            recv_sem=recv_sem.at[j],
            device_id=dev,
            device_id_type=MESH_ID,
        )
        cp.start()
        sends.append(cp)
    own = pltpu.make_async_copy(src.at[me], dst.at[me], local_sem.at[0])
    own.start()
    for j, o in enumerate(offsets):
        s, dev = peer(o, -1)
        pltpu.make_async_remote_copy(
            src_ref=src.at[s],
            dst_ref=dst.at[s],
            send_sem=send_sem.at[j],
            recv_sem=recv_sem.at[j],
            device_id=dev,
            device_id_type=MESH_ID,
        ).wait_recv()
    for cp in sends:
        cp.wait_send()
    own.wait()


def exchange(pieces):
    n = pieces.shape[0]
    return pl.pallas_call(
        exchange_kernel,
        out_shape=jax.ShapeDtypeStruct(pieces.shape, pieces.dtype),
        in_specs=[pl.BlockSpec(memory_space=pl.ANY)],
        out_specs=pl.BlockSpec(memory_space=pl.ANY),
        scratch_shapes=[
            pltpu.SemaphoreType.DMA((n,)),
            pltpu.SemaphoreType.DMA((n,)),
            pltpu.SemaphoreType.DMA((1,)),
        ],
        compiler_params=pltpu.CompilerParams(collective_id=1, has_side_effects=True),
    )(pieces)


def handover_kernel(up_ref, dn_ref, up_out, dn_out, send_sem, recv_sem, fwd_send, fwd_recv, local_sem):
    n_rep = up_out.shape[1]
    n_x = n_rep // 2
    me = lax.axis_index("rep")
    mc = lax.axis_index("mc")
    c = lax.axis_index("core")
    other = 1 - c
    x = lax.div(me, 2)
    zl = lax.rem(me, 2)
    partner = me + 1 - 2 * zl
    xs = [lax.rem(x + d, n_x) * 2 for d in range(1, n_x)]

    barrier = pltpu.get_barrier_semaphore()
    for t in [partner] + [xo + zl for xo in xs]:
        pl.semaphore_signal(barrier, 1, device_id=(t, mc, c), device_id_type=MESH_ID)
    pl.semaphore_signal(barrier, 1, device_id=(me, mc, other), device_id_type=MESH_ID)
    pl.semaphore_wait(barrier, n_x + 1)

    pairs = ((up_ref, up_out), (dn_ref, dn_out))

    def recv_desc(i, slot):
        dst = pairs[i][1]
        return pltpu.make_async_remote_copy(
            src_ref=dst.at[c, slot],
            dst_ref=dst.at[c, slot],
            send_sem=send_sem.at[i, 0],
            recv_sem=recv_sem.at[i, slot],
            device_id=(slot, mc, c),
            device_id_type=MESH_ID,
        )

    locals_ = []
    sends = []
    for i, (src, dst) in enumerate(pairs):
        cp = pltpu.make_async_copy(src, dst.at[c, me], local_sem.at[i])
        cp.start()
        locals_.append(cp)
        for j, t in enumerate([partner] + [xo + zl for xo in xs]):
            cp = pltpu.make_async_remote_copy(
                src_ref=src,
                dst_ref=dst.at[c, me],
                send_sem=send_sem.at[i, j],
                recv_sem=recv_sem.at[i, me],
                device_id=(t, mc, c),
                device_id_type=MESH_ID,
            )
            cp.start()
            sends.append(cp)
    for i, (src, dst) in enumerate(pairs):
        recv_desc(i, partner).wait_recv()
        for j, xo in enumerate(xs):
            cp = pltpu.make_async_remote_copy(
                src_ref=dst.at[c, partner],
                dst_ref=dst.at[c, partner],
                send_sem=send_sem.at[i, n_x + j],
                recv_sem=recv_sem.at[i, partner],
                device_id=(xo + zl, mc, c),
                device_id_type=MESH_ID,
            )
            cp.start()
            sends.append(cp)

    forwards = []
    for i, (src, dst) in enumerate(pairs):
        order = [me, partner] + [xo + zl for xo in xs] + [xo + 1 - zl for xo in xs]
        for slot in order:
            if slot is me:
                locals_[i].wait()
            elif slot is not partner:
                recv_desc(i, slot).wait_recv()
            fw = pltpu.make_async_remote_copy(
                src_ref=dst.at[c, slot],
                dst_ref=dst.at[c, slot],
                send_sem=fwd_send.at[i, slot],
                recv_sem=fwd_recv.at[i, slot],
                device_id=(me, mc, other),
                device_id_type=MESH_ID,
            )
            fw.start()
            forwards.append(fw)

    for cp in sends:
        cp.wait_send()
    for i, (src, dst) in enumerate(pairs):
        for slot in range(n_rep):
            pltpu.make_async_remote_copy(
                src_ref=dst.at[other, slot],
                dst_ref=dst.at[other, slot],
                send_sem=fwd_send.at[i, slot],
                recv_sem=fwd_recv.at[i, slot],
                device_id=(me, mc, other),
                device_id_type=MESH_ID,
            ).wait_recv()
    for fw in forwards:
        fw.wait_send()


def handover(up_blk, dn_blk, n_rep):
    units, width = up_blk.shape
    shape = jax.ShapeDtypeStruct((2, n_rep, units, width), up_blk.dtype)
    return pl.pallas_call(
        handover_kernel,
        out_shape=(shape, shape),
        in_specs=[pl.BlockSpec(memory_space=pl.ANY)] * 2,
        out_specs=(pl.BlockSpec(memory_space=pl.ANY),) * 2,
        scratch_shapes=[
            pltpu.SemaphoreType.DMA((2, n_rep)),
            pltpu.SemaphoreType.DMA((2, n_rep)),
            pltpu.SemaphoreType.DMA((2, n_rep)),
            pltpu.SemaphoreType.DMA((2, n_rep)),
            pltpu.SemaphoreType.DMA((2,)),
        ],
        compiler_params=pltpu.CompilerParams(collective_id=0, has_side_effects=True),
    )(up_blk, dn_blk)


def local(tokens, prompt_ids, modulation, trainer_up, trainer_down):
    as_float = tokens[0].astype(jnp.float32)
    average = jnp.mean(as_float, axis=-1, keepdims=True)
    centred = as_float - average
    variance = jnp.mean(centred * centred, axis=-1, keepdims=True)
    normed = centred / jnp.sqrt(variance + 1e-06)
    prompts_here = modulation.shape[1]
    onehot = (prompt_ids[0][:, None] == jnp.arange(prompts_here, dtype=jnp.int32)[None, :]).astype(
        jnp.float32
    )
    chosen = jnp.einsum("tp,pkd->tkd", onehot, modulation[0], precision=lax.Precision.HIGHEST)
    shift = chosen[:, 0]
    scale = chosen[:, 1]
    gate = chosen[:, 2]
    xin = (normed * (1.0 + scale) + shift).astype(jnp.bfloat16)

    n_mp = lax.psum(1, MP)
    n_rep = lax.psum(1, "rep")
    rows, cols = trainer_up.shape
    piece = cols // n_mp
    both = jnp.stack([trainer_up.astype(jnp.bfloat16).T, trainer_down.astype(jnp.bfloat16)])
    flat = (piece * rows // 120, 120)
    both = exchange(both.reshape(2, n_mp, *flat).transpose(1, 0, 2, 3))
    xin, both = lax.optimization_barrier((xin, both))
    x_all = lax.all_gather(xin, "mc", axis=0, tiled=True)
    both = both.reshape(n_mp, 2, piece, rows).transpose(1, 2, 0, 3)
    both = both.reshape(2, piece, n_mp * rows)
    up_all, dn_all = handover(both[0], both[1], n_rep)
    units = 2 * n_rep * piece
    w_up_t = up_all.reshape(units, n_mp * rows)
    w_down = dn_all.reshape(units, n_mp * rows)

    hidden = jax.nn.gelu(
        lax.dot_general(x_all, w_up_t, (((1,), (1,)), ((), ())), preferred_element_type=jnp.float32),
        approximate=True,
    ).astype(jnp.bfloat16)
    mlp = lax.psum_scatter(
        jnp.dot(hidden, w_down, preferred_element_type=jnp.float32).astype(jnp.bfloat16),
        "mc",
        scatter_dimension=0,
        tiled=True,
    ).astype(jnp.float32)
    result = as_float + gate * mlp
    return result.astype(jnp.bfloat16)[None]


def solution(mesh):
    n_rep, n_mp = mesh.devices.shape
    chips = Mesh(mesh.devices.reshape(n_rep, n_mp // 2, 2), ("rep", "mc", "core"))
    in_specs = (
        P("rep", MP, None),
        P("rep", MP),
        P("rep", None, None, None),
        P(MP, "rep"),
        P("rep", MP),
    )
    out_specs = P("rep", MP, None)
    return jax.shard_map(local, mesh=chips, in_specs=in_specs, out_specs=out_specs, check_vma=False)
```

```python
import functools

import jax
import jax.numpy as jnp
from jax import lax
from jax.experimental import pallas as pl
from jax.experimental.pallas import tpu as pltpu
from jax.sharding import Mesh, PartitionSpec as P

MP = ("mc", "core")
MESH_ID = pl.DeviceIdType.MESH


def _offsets(n_zh, n_y):
    ring = lambda d, n: min(d, n - d)
    offs = [(dz, dy, dc) for dz in range(n_zh) for dy in range(n_y) for dc in range(2) if (dz, dy, dc) != (0, 0, 0)]
    return sorted(offs, key=lambda o: -(2 * ring(o[0], n_zh) + ring(o[1], n_y)))


def exchange_kernel(src, dst, send_sem, recv_sem, local_sem):
    n = src.shape[0]
    n_y = 4
    n_zh = n // (2 * n_y)
    mc = lax.axis_index("mc")
    zh = lax.div(mc, n_y)
    yy = lax.rem(mc, n_y)
    c = lax.axis_index("core")
    me = mc * 2 + c
    r = lax.axis_index("rep")
    offsets = _offsets(n_zh, n_y)

    def peer(o, sign):
        z2 = lax.rem(zh + sign * o[0] + n_zh, n_zh)
        y2 = lax.rem(yy + sign * o[1] + n_y, n_y)
        c2 = lax.rem(c + sign * o[2] + 2, 2)
        return (z2 * n_y + y2) * 2 + c2, (r, z2 * n_y + y2, c2)

    barrier = pltpu.get_barrier_semaphore()
    for o in offsets:
        pl.semaphore_signal(barrier, 1, device_id=peer(o, 1)[1], device_id_type=MESH_ID)
    pl.semaphore_wait(barrier, n - 1)
    sends = []
    for j, o in enumerate(offsets):
        t, dev = peer(o, 1)
        cp = pltpu.make_async_remote_copy(
            src_ref=src.at[t],
            dst_ref=dst.at[me],
            send_sem=send_sem.at[j],
            recv_sem=recv_sem.at[j],
            device_id=dev,
            device_id_type=MESH_ID,
        )
        cp.start()
        sends.append(cp)
    own = pltpu.make_async_copy(src.at[me], dst.at[me], local_sem.at[0])
    own.start()
    for j, o in enumerate(offsets):
        s, dev = peer(o, -1)
        pltpu.make_async_remote_copy(
            src_ref=src.at[s],
            dst_ref=dst.at[s],
            send_sem=send_sem.at[j],
            recv_sem=recv_sem.at[j],
            device_id=dev,
            device_id_type=MESH_ID,
        ).wait_recv()
    for cp in sends:
        cp.wait_send()
    own.wait()


def exchange(pieces):
    n = pieces.shape[0]
    return pl.pallas_call(
        exchange_kernel,
        out_shape=jax.ShapeDtypeStruct(pieces.shape, pieces.dtype),
        in_specs=[pl.BlockSpec(memory_space=pl.ANY)],
        out_specs=pl.BlockSpec(memory_space=pl.ANY),
        scratch_shapes=[
            pltpu.SemaphoreType.DMA((n,)),
            pltpu.SemaphoreType.DMA((n,)),
            pltpu.SemaphoreType.DMA((1,)),
        ],
        compiler_params=pltpu.CompilerParams(collective_id=1, has_side_effects=True),
    )(pieces)


def handover_kernel(up_ref, dn_ref, up_out, dn_out, send_sem, recv_sem, fwd_send, fwd_recv, local_sem):
    n_rep = up_out.shape[1]
    n_x = n_rep // 2
    me = lax.axis_index("rep")
    mc = lax.axis_index("mc")
    c = lax.axis_index("core")
    other = 1 - c
    x = lax.div(me, 2)
    zl = lax.rem(me, 2)
    partner = me + 1 - 2 * zl
    steps = sorted(range(1, n_x), key=lambda d: -min(d, n_x - d))
    xs = [lax.rem(x + d, n_x) * 2 for d in steps]

    barrier = pltpu.get_barrier_semaphore()
    for t in [partner] + [xo + zl for xo in xs]:
        pl.semaphore_signal(barrier, 1, device_id=(t, mc, c), device_id_type=MESH_ID)
    pl.semaphore_signal(barrier, 1, device_id=(me, mc, other), device_id_type=MESH_ID)
    pl.semaphore_wait(barrier, n_x + 1)

    pairs = ((up_ref, up_out), (dn_ref, dn_out))

    def recv_desc(i, slot):
        dst = pairs[i][1]
        return pltpu.make_async_remote_copy(
            src_ref=dst.at[c, slot],
            dst_ref=dst.at[c, slot],
            send_sem=send_sem.at[i, 0],
            recv_sem=recv_sem.at[i, slot],
            device_id=(slot, mc, c),
            device_id_type=MESH_ID,
        )

    locals_ = []
    sends = []
    for i, (src, dst) in enumerate(pairs):
        cp = pltpu.make_async_copy(src, dst.at[c, me], local_sem.at[i])
        cp.start()
        locals_.append(cp)
        for j, t in enumerate([partner] + [xo + zl for xo in xs]):
            cp = pltpu.make_async_remote_copy(
                src_ref=src,
                dst_ref=dst.at[c, me],
                send_sem=send_sem.at[i, j],
                recv_sem=recv_sem.at[i, me],
                device_id=(t, mc, c),
                device_id_type=MESH_ID,
            )
            cp.start()
            sends.append(cp)
    for i, (src, dst) in enumerate(pairs):
        recv_desc(i, partner).wait_recv()
        for j, xo in enumerate(xs):
            cp = pltpu.make_async_remote_copy(
                src_ref=dst.at[c, partner],
                dst_ref=dst.at[c, partner],
                send_sem=send_sem.at[i, n_x + j],
                recv_sem=recv_sem.at[i, partner],
                device_id=(xo + zl, mc, c),
                device_id_type=MESH_ID,
            )
            cp.start()
            sends.append(cp)

    forwards = []
    for i, (src, dst) in enumerate(pairs):
        order = [me, partner] + [xo + zl for xo in xs] + [xo + 1 - zl for xo in xs]
        for slot in order:
            if slot is me:
                locals_[i].wait()
            elif slot is not partner:
                recv_desc(i, slot).wait_recv()
            fw = pltpu.make_async_remote_copy(
                src_ref=dst.at[c, slot],
                dst_ref=dst.at[c, slot],
                send_sem=fwd_send.at[i, slot],
                recv_sem=fwd_recv.at[i, slot],
                device_id=(me, mc, other),
                device_id_type=MESH_ID,
            )
            fw.start()
            forwards.append(fw)

    for cp in sends:
        cp.wait_send()
    for i, (src, dst) in enumerate(pairs):
        for slot in range(n_rep):
            pltpu.make_async_remote_copy(
                src_ref=dst.at[other, slot],
                dst_ref=dst.at[other, slot],
                send_sem=fwd_send.at[i, slot],
                recv_sem=fwd_recv.at[i, slot],
                device_id=(me, mc, other),
                device_id_type=MESH_ID,
            ).wait_recv()
    for fw in forwards:
        fw.wait_send()


def handover(up_blk, dn_blk, n_rep):
    units, width = up_blk.shape
    shape = jax.ShapeDtypeStruct((2, n_rep, units, width), up_blk.dtype)
    return pl.pallas_call(
        handover_kernel,
        out_shape=(shape, shape),
        in_specs=[pl.BlockSpec(memory_space=pl.ANY)] * 2,
        out_specs=(pl.BlockSpec(memory_space=pl.ANY),) * 2,
        scratch_shapes=[
            pltpu.SemaphoreType.DMA((2, n_rep)),
            pltpu.SemaphoreType.DMA((2, n_rep)),
            pltpu.SemaphoreType.DMA((2, n_rep)),
            pltpu.SemaphoreType.DMA((2, n_rep)),
            pltpu.SemaphoreType.DMA((2,)),
        ],
        compiler_params=pltpu.CompilerParams(collective_id=0, has_side_effects=True),
    )(up_blk, dn_blk)


def local(tokens, prompt_ids, modulation, trainer_up, trainer_down):
    as_float = tokens[0].astype(jnp.float32)
    average = jnp.mean(as_float, axis=-1, keepdims=True)
    centred = as_float - average
    variance = jnp.mean(centred * centred, axis=-1, keepdims=True)
    normed = centred / jnp.sqrt(variance + 1e-06)
    prompts_here = modulation.shape[1]
    onehot = (prompt_ids[0][:, None] == jnp.arange(prompts_here, dtype=jnp.int32)[None, :]).astype(
        jnp.float32
    )
    chosen = jnp.einsum("tp,pkd->tkd", onehot, modulation[0], precision=lax.Precision.HIGHEST)
    shift = chosen[:, 0]
    scale = chosen[:, 1]
    gate = chosen[:, 2]
    xin = (normed * (1.0 + scale) + shift).astype(jnp.bfloat16)

    n_mp = lax.psum(1, MP)
    n_rep = lax.psum(1, "rep")
    rows, cols = trainer_up.shape
    piece = cols // n_mp
    both = jnp.stack([trainer_up.astype(jnp.bfloat16).T, trainer_down.astype(jnp.bfloat16)])
    flat = (piece * rows // 120, 120)
    both = exchange(both.reshape(2, n_mp, *flat).transpose(1, 0, 2, 3))
    xin, both = lax.optimization_barrier((xin, both))
    x_all = lax.all_gather(xin, "mc", axis=0, tiled=True)
    both = both.reshape(n_mp, 2, piece, rows).transpose(1, 2, 0, 3)
    both = both.reshape(2, piece, n_mp * rows)
    up_all, dn_all = handover(both[0], both[1], n_rep)
    units = 2 * n_rep * piece
    w_up_t = up_all.reshape(units, n_mp * rows)
    w_down = dn_all.reshape(units, n_mp * rows)

    hidden = jax.nn.gelu(
        lax.dot_general(x_all, w_up_t, (((1,), (1,)), ((), ())), preferred_element_type=jnp.float32),
        approximate=True,
    ).astype(jnp.bfloat16)
    mlp = lax.psum_scatter(
        jnp.dot(hidden, w_down, preferred_element_type=jnp.float32).astype(jnp.bfloat16),
        "mc",
        scatter_dimension=0,
        tiled=True,
    ).astype(jnp.float32)
    result = as_float + gate * mlp
    return result.astype(jnp.bfloat16)[None]


def solution(mesh):
    n_rep, n_mp = mesh.devices.shape
    chips = Mesh(mesh.devices.reshape(n_rep, n_mp // 2, 2), ("rep", "mc", "core"))
    in_specs = (
        P("rep", MP, None),
        P("rep", MP),
        P("rep", None, None, None),
        P(MP, "rep"),
        P("rep", MP),
    )
    out_specs = P("rep", MP, None)
    return jax.shard_map(local, mesh=chips, in_specs=in_specs, out_specs=out_specs, check_vma=False)
```

```python
import functools

import jax
import jax.numpy as jnp
from jax import lax
from jax.experimental import pallas as pl
from jax.experimental.pallas import tpu as pltpu
from jax.sharding import Mesh, PartitionSpec as P

MP = ("mc", "core")
MESH_ID = pl.DeviceIdType.MESH


def _offsets(n_zh, n_y):
    ring = lambda d, n: min(d, n - d)
    offs = [(dz, dy, dc) for dz in range(n_zh) for dy in range(n_y) for dc in range(2) if (dz, dy, dc) != (0, 0, 0)]
    return sorted(offs, key=lambda o: -(2 * ring(o[0], n_zh) + ring(o[1], n_y)))


def modulate(tok_ref, ids_ref, mod_ref, xin_ref, gate_ref):
    x = tok_ref[...].astype(jnp.float32)
    average = jnp.mean(x, axis=-1, keepdims=True)
    centred = x - average
    variance = jnp.mean(centred * centred, axis=-1, keepdims=True)
    normed = centred / jnp.sqrt(variance + 1e-06)
    ids = ids_ref[...]
    shift = jnp.zeros_like(normed)
    scale = jnp.zeros_like(normed)
    gate = jnp.zeros_like(normed)
    for p in range(mod_ref.shape[0] // 3):
        hit = ids == p
        shift = jnp.where(hit, mod_ref[pl.ds(3 * p, 1), :], shift)
        scale = jnp.where(hit, mod_ref[pl.ds(3 * p + 1, 1), :], scale)
        gate = jnp.where(hit, mod_ref[pl.ds(3 * p + 2, 1), :], gate)
    xin_ref[...] = (normed * (1.0 + scale) + shift).astype(xin_ref.dtype)
    gate_ref[...] = gate


def exchange_kernel(src, tok_ref, ids_ref, mod_ref, dst, xin_ref, gate_ref, send_sem, recv_sem, local_sem):
    n = src.shape[0]
    n_y = 4
    n_zh = n // (2 * n_y)
    mc = lax.axis_index("mc")
    zh = lax.div(mc, n_y)
    yy = lax.rem(mc, n_y)
    c = lax.axis_index("core")
    me = mc * 2 + c
    r = lax.axis_index("rep")
    offsets = _offsets(n_zh, n_y)

    def peer(o, sign):
        z2 = lax.rem(zh + sign * o[0] + n_zh, n_zh)
        y2 = lax.rem(yy + sign * o[1] + n_y, n_y)
        c2 = lax.rem(c + sign * o[2] + 2, 2)
        return (z2 * n_y + y2) * 2 + c2, (r, z2 * n_y + y2, c2)

    barrier = pltpu.get_barrier_semaphore()
    for o in offsets:
        pl.semaphore_signal(barrier, 1, device_id=peer(o, 1)[1], device_id_type=MESH_ID)
    pl.semaphore_wait(barrier, n - 1)
    sends = []
    for j, o in enumerate(offsets):
        t, dev = peer(o, 1)
        cp = pltpu.make_async_remote_copy(
            src_ref=src.at[t],
            dst_ref=dst.at[me],
            send_sem=send_sem.at[j],
            recv_sem=recv_sem.at[j],
            device_id=dev,
            device_id_type=MESH_ID,
        )
        cp.start()
        sends.append(cp)
    own = pltpu.make_async_copy(src.at[me], dst.at[me], local_sem.at[0])
    own.start()
    modulate(tok_ref, ids_ref, mod_ref, xin_ref, gate_ref)
    for j, o in enumerate(offsets):
        s, dev = peer(o, -1)
        pltpu.make_async_remote_copy(
            src_ref=src.at[s],
            dst_ref=dst.at[s],
            send_sem=send_sem.at[j],
            recv_sem=recv_sem.at[j],
            device_id=dev,
            device_id_type=MESH_ID,
        ).wait_recv()
    for cp in sends:
        cp.wait_send()
    own.wait()


def exchange(pieces, tokens, ids, mod):
    n = pieces.shape[0]
    vmem = pl.BlockSpec(memory_space=pltpu.VMEM)
    return pl.pallas_call(
        exchange_kernel,
        out_shape=(
            jax.ShapeDtypeStruct(pieces.shape, pieces.dtype),
            jax.ShapeDtypeStruct(tokens.shape, jnp.bfloat16),
            jax.ShapeDtypeStruct(tokens.shape, jnp.float32),
        ),
        in_specs=[pl.BlockSpec(memory_space=pl.ANY), vmem, vmem, vmem],
        out_specs=(pl.BlockSpec(memory_space=pl.ANY), vmem, vmem),
        scratch_shapes=[
            pltpu.SemaphoreType.DMA((n,)),
            pltpu.SemaphoreType.DMA((n,)),
            pltpu.SemaphoreType.DMA((1,)),
        ],
        compiler_params=pltpu.CompilerParams(collective_id=1, has_side_effects=True),
    )(pieces, tokens, ids, mod)


def handover_kernel(up_ref, dn_ref, up_out, dn_out, send_sem, recv_sem, fwd_send, fwd_recv, local_sem):
    n_rep = up_out.shape[1]
    n_x = n_rep // 2
    me = lax.axis_index("rep")
    mc = lax.axis_index("mc")
    c = lax.axis_index("core")
    other = 1 - c
    x = lax.div(me, 2)
    zl = lax.rem(me, 2)
    partner = me + 1 - 2 * zl
    xs = [lax.rem(x + d, n_x) * 2 for d in range(1, n_x)]

    barrier = pltpu.get_barrier_semaphore()
    for t in [partner] + [xo + zl for xo in xs]:
        pl.semaphore_signal(barrier, 1, device_id=(t, mc, c), device_id_type=MESH_ID)
    pl.semaphore_signal(barrier, 1, device_id=(me, mc, other), device_id_type=MESH_ID)
    pl.semaphore_wait(barrier, n_x + 1)

    pairs = ((up_ref, up_out), (dn_ref, dn_out))

    def recv_desc(i, slot):
        dst = pairs[i][1]
        return pltpu.make_async_remote_copy(
            src_ref=dst.at[c, slot],
            dst_ref=dst.at[c, slot],
            send_sem=send_sem.at[i, 0],
            recv_sem=recv_sem.at[i, slot],
            device_id=(slot, mc, c),
            device_id_type=MESH_ID,
        )

    locals_ = []
    sends = []
    for i, (src, dst) in enumerate(pairs):
        cp = pltpu.make_async_copy(src, dst.at[c, me], local_sem.at[i])
        cp.start()
        locals_.append(cp)
        for j, t in enumerate([partner] + [xo + zl for xo in xs]):
            cp = pltpu.make_async_remote_copy(
                src_ref=src,
                dst_ref=dst.at[c, me],
                send_sem=send_sem.at[i, j],
                recv_sem=recv_sem.at[i, me],
                device_id=(t, mc, c),
                device_id_type=MESH_ID,
            )
            cp.start()
            sends.append(cp)
    for i, (src, dst) in enumerate(pairs):
        recv_desc(i, partner).wait_recv()
        for j, xo in enumerate(xs):
            cp = pltpu.make_async_remote_copy(
                src_ref=dst.at[c, partner],
                dst_ref=dst.at[c, partner],
                send_sem=send_sem.at[i, n_x + j],
                recv_sem=recv_sem.at[i, partner],
                device_id=(xo + zl, mc, c),
                device_id_type=MESH_ID,
            )
            cp.start()
            sends.append(cp)

    forwards = []
    for i, (src, dst) in enumerate(pairs):
        order = [me, partner] + [xo + zl for xo in xs] + [xo + 1 - zl for xo in xs]
        for slot in order:
            if slot is me:
                locals_[i].wait()
            elif slot is not partner:
                recv_desc(i, slot).wait_recv()
            fw = pltpu.make_async_remote_copy(
                src_ref=dst.at[c, slot],
                dst_ref=dst.at[c, slot],
                send_sem=fwd_send.at[i, slot],
                recv_sem=fwd_recv.at[i, slot],
                device_id=(me, mc, other),
                device_id_type=MESH_ID,
            )
            fw.start()
            forwards.append(fw)

    for cp in sends:
        cp.wait_send()
    for i, (src, dst) in enumerate(pairs):
        for slot in range(n_rep):
            pltpu.make_async_remote_copy(
                src_ref=dst.at[other, slot],
                dst_ref=dst.at[other, slot],
                send_sem=fwd_send.at[i, slot],
                recv_sem=fwd_recv.at[i, slot],
                device_id=(me, mc, other),
                device_id_type=MESH_ID,
            ).wait_recv()
    for fw in forwards:
        fw.wait_send()


def handover(up_blk, dn_blk, n_rep):
    units, width = up_blk.shape
    shape = jax.ShapeDtypeStruct((2, n_rep, units, width), up_blk.dtype)
    return pl.pallas_call(
        handover_kernel,
        out_shape=(shape, shape),
        in_specs=[pl.BlockSpec(memory_space=pl.ANY)] * 2,
        out_specs=(pl.BlockSpec(memory_space=pl.ANY),) * 2,
        scratch_shapes=[
            pltpu.SemaphoreType.DMA((2, n_rep)),
            pltpu.SemaphoreType.DMA((2, n_rep)),
            pltpu.SemaphoreType.DMA((2, n_rep)),
            pltpu.SemaphoreType.DMA((2, n_rep)),
            pltpu.SemaphoreType.DMA((2,)),
        ],
        compiler_params=pltpu.CompilerParams(collective_id=0, has_side_effects=True),
    )(up_blk, dn_blk)


def local(tokens, prompt_ids, modulation, trainer_up, trainer_down):
    as_float = tokens[0].astype(jnp.float32)
    n_mp = lax.psum(1, MP)
    n_rep = lax.psum(1, "rep")
    rows, cols = trainer_up.shape
    piece = cols // n_mp
    both = jnp.stack([trainer_up.astype(jnp.bfloat16).T, trainer_down.astype(jnp.bfloat16)])
    flat = (piece * rows // 120, 120)
    mod = modulation[0].reshape(-1, modulation.shape[-1])
    both, xin, gate = exchange(
        both.reshape(2, n_mp, *flat).transpose(1, 0, 2, 3), tokens[0], prompt_ids[0][:, None], mod
    )
    x_all = lax.all_gather(xin, "mc", axis=0, tiled=True)
    both = both.reshape(n_mp, 2, piece, rows).transpose(1, 2, 0, 3)
    both = both.reshape(2, piece, n_mp * rows)
    up_all, dn_all = handover(both[0], both[1], n_rep)
    units = 2 * n_rep * piece
    w_up_t = up_all.reshape(units, n_mp * rows)
    w_down = dn_all.reshape(units, n_mp * rows)

    hidden = jax.nn.gelu(
        lax.dot_general(x_all, w_up_t, (((1,), (1,)), ((), ())), preferred_element_type=jnp.float32),
        approximate=True,
    ).astype(jnp.bfloat16)
    mlp = lax.psum_scatter(
        jnp.dot(hidden, w_down, preferred_element_type=jnp.float32).astype(jnp.bfloat16),
        "mc",
        scatter_dimension=0,
        tiled=True,
    ).astype(jnp.float32)
    result = as_float + gate * mlp
    return result.astype(jnp.bfloat16)[None]


def solution(mesh):
    n_rep, n_mp = mesh.devices.shape
    chips = Mesh(mesh.devices.reshape(n_rep, n_mp // 2, 2), ("rep", "mc", "core"))
    in_specs = (
        P("rep", MP, None),
        P("rep", MP),
        P("rep", None, None, None),
        P(MP, "rep"),
        P("rep", MP),
    )
    out_specs = P("rep", MP, None)
    return jax.shard_map(local, mesh=chips, in_specs=in_specs, out_specs=out_specs, check_vma=False)
```

```python
import functools

import jax
import jax.numpy as jnp
from jax import lax
from jax.experimental import pallas as pl
from jax.experimental.pallas import tpu as pltpu
from jax.sharding import Mesh, PartitionSpec as P

MP = ("mc", "core")
MESH_ID = pl.DeviceIdType.MESH


def _offsets(n_zh, n_y):
    ring = lambda d, n: min(d, n - d)
    offs = [(dz, dy, dc) for dz in range(n_zh) for dy in range(n_y) for dc in range(2) if (dz, dy, dc) != (0, 0, 0)]
    return sorted(offs, key=lambda o: -(2 * ring(o[0], n_zh) + ring(o[1], n_y)))


def modulate(tok_ref, ids_ref, mod_ref, xin_ref, gate_ref):
    x = tok_ref[...].astype(jnp.float32)
    average = jnp.mean(x, axis=-1, keepdims=True)
    centred = x - average
    variance = jnp.mean(centred * centred, axis=-1, keepdims=True)
    normed = centred / jnp.sqrt(variance + 1e-06)
    ids = ids_ref[...]
    shift = jnp.zeros_like(normed)
    scale = jnp.zeros_like(normed)
    gate = jnp.zeros_like(normed)
    for p in range(mod_ref.shape[1]):
        hit = ids == p
        shift = jnp.where(hit, mod_ref[0, p, pl.ds(0, 1), :], shift)
        scale = jnp.where(hit, mod_ref[0, p, pl.ds(1, 1), :], scale)
        gate = jnp.where(hit, mod_ref[0, p, pl.ds(2, 1), :], gate)
    xin_ref[...] = (normed * (1.0 + scale) + shift).astype(xin_ref.dtype)
    gate_ref[...] = gate


def exchange_kernel(src, tok_ref, ids_ref, mod_ref, dst, xin_ref, gate_ref, send_sem, recv_sem, local_sem):
    n = src.shape[0]
    n_y = 4
    n_zh = n // (2 * n_y)
    mc = lax.axis_index("mc")
    zh = lax.div(mc, n_y)
    yy = lax.rem(mc, n_y)
    c = lax.axis_index("core")
    me = mc * 2 + c
    r = lax.axis_index("rep")
    offsets = _offsets(n_zh, n_y)

    def peer(o, sign):
        z2 = lax.rem(zh + sign * o[0] + n_zh, n_zh)
        y2 = lax.rem(yy + sign * o[1] + n_y, n_y)
        c2 = lax.rem(c + sign * o[2] + 2, 2)
        return (z2 * n_y + y2) * 2 + c2, (r, z2 * n_y + y2, c2)

    barrier = pltpu.get_barrier_semaphore()
    for o in offsets:
        pl.semaphore_signal(barrier, 1, device_id=peer(o, 1)[1], device_id_type=MESH_ID)
    pl.semaphore_wait(barrier, n - 1)
    sends = []
    for j, o in enumerate(offsets):
        t, dev = peer(o, 1)
        cp = pltpu.make_async_remote_copy(
            src_ref=src.at[t],
            dst_ref=dst.at[me],
            send_sem=send_sem.at[j],
            recv_sem=recv_sem.at[j],
            device_id=dev,
            device_id_type=MESH_ID,
        )
        cp.start()
        sends.append(cp)
    own = pltpu.make_async_copy(src.at[me], dst.at[me], local_sem.at[0])
    own.start()
    modulate(tok_ref, ids_ref, mod_ref, xin_ref, gate_ref)
    for j, o in enumerate(offsets):
        s, dev = peer(o, -1)
        pltpu.make_async_remote_copy(
            src_ref=src.at[s],
            dst_ref=dst.at[s],
            send_sem=send_sem.at[j],
            recv_sem=recv_sem.at[j],
            device_id=dev,
            device_id_type=MESH_ID,
        ).wait_recv()
    for cp in sends:
        cp.wait_send()
    own.wait()


def exchange(pieces, tokens, ids, mod):
    n = pieces.shape[0]
    vmem = pl.BlockSpec(memory_space=pltpu.VMEM)
    return pl.pallas_call(
        exchange_kernel,
        out_shape=(
            jax.ShapeDtypeStruct(pieces.shape, pieces.dtype),
            jax.ShapeDtypeStruct(tokens.shape, jnp.bfloat16),
            jax.ShapeDtypeStruct(tokens.shape, jnp.float32),
        ),
        in_specs=[pl.BlockSpec(memory_space=pl.ANY), vmem, vmem, vmem],
        out_specs=(pl.BlockSpec(memory_space=pl.ANY), vmem, vmem),
        scratch_shapes=[
            pltpu.SemaphoreType.DMA((n,)),
            pltpu.SemaphoreType.DMA((n,)),
            pltpu.SemaphoreType.DMA((1,)),
        ],
        compiler_params=pltpu.CompilerParams(collective_id=1, has_side_effects=True),
    )(pieces, tokens, ids, mod)


def handover_kernel(up_ref, dn_ref, up_out, dn_out, send_sem, recv_sem, fwd_send, fwd_recv, local_sem):
    n_rep = up_out.shape[1]
    n_x = n_rep // 2
    me = lax.axis_index("rep")
    mc = lax.axis_index("mc")
    c = lax.axis_index("core")
    other = 1 - c
    x = lax.div(me, 2)
    zl = lax.rem(me, 2)
    partner = me + 1 - 2 * zl
    xs = [lax.rem(x + d, n_x) * 2 for d in range(1, n_x)]

    barrier = pltpu.get_barrier_semaphore()
    for t in [partner] + [xo + zl for xo in xs]:
        pl.semaphore_signal(barrier, 1, device_id=(t, mc, c), device_id_type=MESH_ID)
    pl.semaphore_signal(barrier, 1, device_id=(me, mc, other), device_id_type=MESH_ID)
    pl.semaphore_wait(barrier, n_x + 1)

    pairs = ((up_ref, up_out), (dn_ref, dn_out))

    def recv_desc(i, slot):
        dst = pairs[i][1]
        return pltpu.make_async_remote_copy(
            src_ref=dst.at[c, slot],
            dst_ref=dst.at[c, slot],
            send_sem=send_sem.at[i, 0],
            recv_sem=recv_sem.at[i, slot],
            device_id=(slot, mc, c),
            device_id_type=MESH_ID,
        )

    locals_ = []
    sends = []
    for i, (src, dst) in enumerate(pairs):
        cp = pltpu.make_async_copy(src, dst.at[c, me], local_sem.at[i])
        cp.start()
        locals_.append(cp)
        for j, t in enumerate([partner] + [xo + zl for xo in xs]):
            cp = pltpu.make_async_remote_copy(
                src_ref=src,
                dst_ref=dst.at[c, me],
                send_sem=send_sem.at[i, j],
                recv_sem=recv_sem.at[i, me],
                device_id=(t, mc, c),
                device_id_type=MESH_ID,
            )
            cp.start()
            sends.append(cp)
    for i, (src, dst) in enumerate(pairs):
        recv_desc(i, partner).wait_recv()
        for j, xo in enumerate(xs):
            cp = pltpu.make_async_remote_copy(
                src_ref=dst.at[c, partner],
                dst_ref=dst.at[c, partner],
                send_sem=send_sem.at[i, n_x + j],
                recv_sem=recv_sem.at[i, partner],
                device_id=(xo + zl, mc, c),
                device_id_type=MESH_ID,
            )
            cp.start()
            sends.append(cp)

    forwards = []
    for i, (src, dst) in enumerate(pairs):
        order = [me, partner] + [xo + zl for xo in xs] + [xo + 1 - zl for xo in xs]
        for slot in order:
            if slot is me:
                locals_[i].wait()
            elif slot is not partner:
                recv_desc(i, slot).wait_recv()
            fw = pltpu.make_async_remote_copy(
                src_ref=dst.at[c, slot],
                dst_ref=dst.at[c, slot],
                send_sem=fwd_send.at[i, slot],
                recv_sem=fwd_recv.at[i, slot],
                device_id=(me, mc, other),
                device_id_type=MESH_ID,
            )
            fw.start()
            forwards.append(fw)

    for cp in sends:
        cp.wait_send()
    for i, (src, dst) in enumerate(pairs):
        for slot in range(n_rep):
            pltpu.make_async_remote_copy(
                src_ref=dst.at[other, slot],
                dst_ref=dst.at[other, slot],
                send_sem=fwd_send.at[i, slot],
                recv_sem=fwd_recv.at[i, slot],
                device_id=(me, mc, other),
                device_id_type=MESH_ID,
            ).wait_recv()
    for fw in forwards:
        fw.wait_send()


def handover(up_blk, dn_blk, n_rep):
    units, width = up_blk.shape
    shape = jax.ShapeDtypeStruct((2, n_rep, units, width), up_blk.dtype)
    return pl.pallas_call(
        handover_kernel,
        out_shape=(shape, shape),
        in_specs=[pl.BlockSpec(memory_space=pl.ANY)] * 2,
        out_specs=(pl.BlockSpec(memory_space=pl.ANY),) * 2,
        scratch_shapes=[
            pltpu.SemaphoreType.DMA((2, n_rep)),
            pltpu.SemaphoreType.DMA((2, n_rep)),
            pltpu.SemaphoreType.DMA((2, n_rep)),
            pltpu.SemaphoreType.DMA((2, n_rep)),
            pltpu.SemaphoreType.DMA((2,)),
        ],
        compiler_params=pltpu.CompilerParams(collective_id=0, has_side_effects=True),
    )(up_blk, dn_blk)


def local(tokens, prompt_ids, modulation, trainer_up, trainer_down):
    as_float = tokens[0].astype(jnp.float32)
    n_mp = lax.psum(1, MP)
    n_rep = lax.psum(1, "rep")
    rows, cols = trainer_up.shape
    piece = cols // n_mp
    both = jnp.stack([trainer_up.astype(jnp.bfloat16).T, trainer_down.astype(jnp.bfloat16)])
    flat = (piece * rows // 120, 120)
    both, xin, gate = exchange(
        both.reshape(2, n_mp, *flat).transpose(1, 0, 2, 3), tokens[0], prompt_ids[0][:, None], modulation
    )
    x_all = lax.all_gather(xin, "mc", axis=0, tiled=True)
    both = both.reshape(n_mp, 2, piece, rows).transpose(1, 2, 0, 3)
    both = both.reshape(2, piece, n_mp * rows)
    up_all, dn_all = handover(both[0], both[1], n_rep)
    units = 2 * n_rep * piece
    w_up_t = up_all.reshape(units, n_mp * rows)
    w_down = dn_all.reshape(units, n_mp * rows)

    hidden = jax.nn.gelu(
        lax.dot_general(x_all, w_up_t, (((1,), (1,)), ((), ())), preferred_element_type=jnp.float32),
        approximate=True,
    ).astype(jnp.bfloat16)
    mlp = lax.psum_scatter(
        jnp.dot(hidden, w_down, preferred_element_type=jnp.float32).astype(jnp.bfloat16),
        "mc",
        scatter_dimension=0,
        tiled=True,
    ).astype(jnp.float32)
    result = as_float + gate * mlp
    return result.astype(jnp.bfloat16)[None]


def solution(mesh):
    n_rep, n_mp = mesh.devices.shape
    chips = Mesh(mesh.devices.reshape(n_rep, n_mp // 2, 2), ("rep", "mc", "core"))
    in_specs = (
        P("rep", MP, None),
        P("rep", MP),
        P("rep", None, None, None),
        P(MP, "rep"),
        P("rep", MP),
    )
    out_specs = P("rep", MP, None)
    return jax.shard_map(local, mesh=chips, in_specs=in_specs, out_specs=out_specs, check_vma=False)
```

```python
import functools

import jax
import jax.numpy as jnp
from jax import lax
from jax.experimental import pallas as pl
from jax.experimental.pallas import tpu as pltpu
from jax.sharding import Mesh, PartitionSpec as P

MP = ("mc", "core")
MESH_ID = pl.DeviceIdType.MESH


def _offsets(n_zh, n_y):
    ring = lambda d, n: min(d, n - d)
    offs = [(dz, dy, dc) for dz in range(n_zh) for dy in range(n_y) for dc in range(2) if (dz, dy, dc) != (0, 0, 0)]
    return sorted(offs, key=lambda o: -(2 * ring(o[0], n_zh) + ring(o[1], n_y)))


def modulate(tok_ref, ids_ref, mod_ref, xin_ref, gate_ref):
    x = tok_ref[...].astype(jnp.float32)
    average = jnp.mean(x, axis=-1, keepdims=True)
    centred = x - average
    variance = jnp.mean(centred * centred, axis=-1, keepdims=True)
    normed = centred / jnp.sqrt(variance + 1e-06)
    prompts = mod_ref.shape[1]
    onehot = (ids_ref[...] == lax.broadcasted_iota(jnp.int32, (1, prompts), 1)).astype(jnp.float32)

    def pick(k):
        rows = mod_ref[0, :, pl.ds(k, 1), :].reshape(prompts, -1)
        return jnp.dot(onehot, rows, precision=lax.Precision.HIGHEST, preferred_element_type=jnp.float32)

    shift, scale, gate = pick(0), pick(1), pick(2)
    xin_ref[...] = (normed * (1.0 + scale) + shift).astype(xin_ref.dtype)
    gate_ref[...] = gate


def exchange_kernel(src, tok_ref, ids_ref, mod_ref, dst, xin_ref, gate_ref, send_sem, recv_sem, local_sem):
    n = src.shape[0]
    n_y = 4
    n_zh = n // (2 * n_y)
    mc = lax.axis_index("mc")
    zh = lax.div(mc, n_y)
    yy = lax.rem(mc, n_y)
    c = lax.axis_index("core")
    me = mc * 2 + c
    r = lax.axis_index("rep")
    offsets = _offsets(n_zh, n_y)

    def peer(o, sign):
        z2 = lax.rem(zh + sign * o[0] + n_zh, n_zh)
        y2 = lax.rem(yy + sign * o[1] + n_y, n_y)
        c2 = lax.rem(c + sign * o[2] + 2, 2)
        return (z2 * n_y + y2) * 2 + c2, (r, z2 * n_y + y2, c2)

    barrier = pltpu.get_barrier_semaphore()
    for o in offsets:
        pl.semaphore_signal(barrier, 1, device_id=peer(o, 1)[1], device_id_type=MESH_ID)
    pl.semaphore_wait(barrier, n - 1)
    sends = []
    for j, o in enumerate(offsets):
        t, dev = peer(o, 1)
        cp = pltpu.make_async_remote_copy(
            src_ref=src.at[t],
            dst_ref=dst.at[me],
            send_sem=send_sem.at[j],
            recv_sem=recv_sem.at[j],
            device_id=dev,
            device_id_type=MESH_ID,
        )
        cp.start()
        sends.append(cp)
    own = pltpu.make_async_copy(src.at[me], dst.at[me], local_sem.at[0])
    own.start()
    modulate(tok_ref, ids_ref, mod_ref, xin_ref, gate_ref)
    for j, o in enumerate(offsets):
        s, dev = peer(o, -1)
        pltpu.make_async_remote_copy(
            src_ref=src.at[s],
            dst_ref=dst.at[s],
            send_sem=send_sem.at[j],
            recv_sem=recv_sem.at[j],
            device_id=dev,
            device_id_type=MESH_ID,
        ).wait_recv()
    for cp in sends:
        cp.wait_send()
    own.wait()


def exchange(pieces, tokens, ids, mod):
    n = pieces.shape[0]
    vmem = pl.BlockSpec(memory_space=pltpu.VMEM)
    return pl.pallas_call(
        exchange_kernel,
        out_shape=(
            jax.ShapeDtypeStruct(pieces.shape, pieces.dtype),
            jax.ShapeDtypeStruct(tokens.shape, jnp.bfloat16),
            jax.ShapeDtypeStruct(tokens.shape, jnp.float32),
        ),
        in_specs=[pl.BlockSpec(memory_space=pl.ANY), vmem, vmem, vmem],
        out_specs=(pl.BlockSpec(memory_space=pl.ANY), vmem, vmem),
        scratch_shapes=[
            pltpu.SemaphoreType.DMA((n,)),
            pltpu.SemaphoreType.DMA((n,)),
            pltpu.SemaphoreType.DMA((1,)),
        ],
        compiler_params=pltpu.CompilerParams(collective_id=1, has_side_effects=True),
    )(pieces, tokens, ids, mod)


def handover_kernel(up_ref, dn_ref, up_out, dn_out, send_sem, recv_sem, fwd_send, fwd_recv, local_sem):
    n_rep = up_out.shape[1]
    n_x = n_rep // 2
    me = lax.axis_index("rep")
    mc = lax.axis_index("mc")
    c = lax.axis_index("core")
    other = 1 - c
    x = lax.div(me, 2)
    zl = lax.rem(me, 2)
    partner = me + 1 - 2 * zl
    xs = [lax.rem(x + d, n_x) * 2 for d in range(1, n_x)]

    barrier = pltpu.get_barrier_semaphore()
    for t in [partner] + [xo + zl for xo in xs]:
        pl.semaphore_signal(barrier, 1, device_id=(t, mc, c), device_id_type=MESH_ID)
    pl.semaphore_signal(barrier, 1, device_id=(me, mc, other), device_id_type=MESH_ID)
    pl.semaphore_wait(barrier, n_x + 1)

    pairs = ((up_ref, up_out), (dn_ref, dn_out))

    def recv_desc(i, slot):
        dst = pairs[i][1]
        return pltpu.make_async_remote_copy(
            src_ref=dst.at[c, slot],
            dst_ref=dst.at[c, slot],
            send_sem=send_sem.at[i, 0],
            recv_sem=recv_sem.at[i, slot],
            device_id=(slot, mc, c),
            device_id_type=MESH_ID,
        )

    locals_ = []
    sends = []
    for i, (src, dst) in enumerate(pairs):
        cp = pltpu.make_async_copy(src, dst.at[c, me], local_sem.at[i])
        cp.start()
        locals_.append(cp)
        for j, t in enumerate([partner] + [xo + zl for xo in xs]):
            cp = pltpu.make_async_remote_copy(
                src_ref=src,
                dst_ref=dst.at[c, me],
                send_sem=send_sem.at[i, j],
                recv_sem=recv_sem.at[i, me],
                device_id=(t, mc, c),
                device_id_type=MESH_ID,
            )
            cp.start()
            sends.append(cp)
    for i, (src, dst) in enumerate(pairs):
        recv_desc(i, partner).wait_recv()
        for j, xo in enumerate(xs):
            cp = pltpu.make_async_remote_copy(
                src_ref=dst.at[c, partner],
                dst_ref=dst.at[c, partner],
                send_sem=send_sem.at[i, n_x + j],
                recv_sem=recv_sem.at[i, partner],
                device_id=(xo + zl, mc, c),
                device_id_type=MESH_ID,
            )
            cp.start()
            sends.append(cp)

    forwards = []
    for i, (src, dst) in enumerate(pairs):
        order = [me, partner] + [xo + zl for xo in xs] + [xo + 1 - zl for xo in xs]
        for slot in order:
            if slot is me:
                locals_[i].wait()
            elif slot is not partner:
                recv_desc(i, slot).wait_recv()
            fw = pltpu.make_async_remote_copy(
                src_ref=dst.at[c, slot],
                dst_ref=dst.at[c, slot],
                send_sem=fwd_send.at[i, slot],
                recv_sem=fwd_recv.at[i, slot],
                device_id=(me, mc, other),
                device_id_type=MESH_ID,
            )
            fw.start()
            forwards.append(fw)

    for cp in sends:
        cp.wait_send()
    for i, (src, dst) in enumerate(pairs):
        for slot in range(n_rep):
            pltpu.make_async_remote_copy(
                src_ref=dst.at[other, slot],
                dst_ref=dst.at[other, slot],
                send_sem=fwd_send.at[i, slot],
                recv_sem=fwd_recv.at[i, slot],
                device_id=(me, mc, other),
                device_id_type=MESH_ID,
            ).wait_recv()
    for fw in forwards:
        fw.wait_send()


def handover(up_blk, dn_blk, n_rep):
    units, width = up_blk.shape
    shape = jax.ShapeDtypeStruct((2, n_rep, units, width), up_blk.dtype)
    return pl.pallas_call(
        handover_kernel,
        out_shape=(shape, shape),
        in_specs=[pl.BlockSpec(memory_space=pl.ANY)] * 2,
        out_specs=(pl.BlockSpec(memory_space=pl.ANY),) * 2,
        scratch_shapes=[
            pltpu.SemaphoreType.DMA((2, n_rep)),
            pltpu.SemaphoreType.DMA((2, n_rep)),
            pltpu.SemaphoreType.DMA((2, n_rep)),
            pltpu.SemaphoreType.DMA((2, n_rep)),
            pltpu.SemaphoreType.DMA((2,)),
        ],
        compiler_params=pltpu.CompilerParams(collective_id=0, has_side_effects=True),
    )(up_blk, dn_blk)


def local(tokens, prompt_ids, modulation, trainer_up, trainer_down):
    as_float = tokens[0].astype(jnp.float32)
    n_mp = lax.psum(1, MP)
    n_rep = lax.psum(1, "rep")
    rows, cols = trainer_up.shape
    piece = cols // n_mp
    both = jnp.stack([trainer_up.astype(jnp.bfloat16).T, trainer_down.astype(jnp.bfloat16)])
    flat = (piece * rows // 120, 120)
    both, xin, gate = exchange(
        both.reshape(2, n_mp, *flat).transpose(1, 0, 2, 3), tokens[0], prompt_ids[0][:, None], modulation
    )
    x_all = lax.all_gather(xin, "mc", axis=0, tiled=True)
    both = both.reshape(n_mp, 2, piece, rows).transpose(1, 2, 0, 3)
    both = both.reshape(2, piece, n_mp * rows)
    up_all, dn_all = handover(both[0], both[1], n_rep)
    units = 2 * n_rep * piece
    w_up_t = up_all.reshape(units, n_mp * rows)
    w_down = dn_all.reshape(units, n_mp * rows)

    hidden = jax.nn.gelu(
        lax.dot_general(x_all, w_up_t, (((1,), (1,)), ((), ())), preferred_element_type=jnp.float32),
        approximate=True,
    ).astype(jnp.bfloat16)
    mlp = lax.psum_scatter(
        jnp.dot(hidden, w_down, preferred_element_type=jnp.float32).astype(jnp.bfloat16),
        "mc",
        scatter_dimension=0,
        tiled=True,
    ).astype(jnp.float32)
    result = as_float + gate * mlp
    return result.astype(jnp.bfloat16)[None]


def solution(mesh):
    n_rep, n_mp = mesh.devices.shape
    chips = Mesh(mesh.devices.reshape(n_rep, n_mp // 2, 2), ("rep", "mc", "core"))
    in_specs = (
        P("rep", MP, None),
        P("rep", MP),
        P("rep", None, None, None),
        P(MP, "rep"),
        P("rep", MP),
    )
    out_specs = P("rep", MP, None)
    return jax.shard_map(local, mesh=chips, in_specs=in_specs, out_specs=out_specs, check_vma=False)
```

```python
import functools

import jax
import jax.numpy as jnp
from jax import lax
from jax.experimental import pallas as pl
from jax.experimental.pallas import tpu as pltpu
from jax.sharding import Mesh, PartitionSpec as P

MP = ("mc", "core")
MESH_ID = pl.DeviceIdType.MESH


def _offsets(n_zh, n_y):
    ring = lambda d, n: min(d, n - d)
    offs = [(dz, dy, dc) for dz in range(n_zh) for dy in range(n_y) for dc in range(2) if (dz, dy, dc) != (0, 0, 0)]
    return sorted(offs, key=lambda o: -(2 * ring(o[0], n_zh) + ring(o[1], n_y)))


def modulate(tok_ref, ids_ref, mod_ref, xin_ref, gate_ref):
    x = tok_ref[...].astype(jnp.float32)
    average = jnp.mean(x, axis=-1, keepdims=True)
    centred = x - average
    variance = jnp.mean(centred * centred, axis=-1, keepdims=True)
    normed = centred / jnp.sqrt(variance + 1e-06)
    prompts = mod_ref.shape[1]
    onehot_t = (lax.broadcasted_iota(jnp.int32, (prompts, 1), 0) == ids_ref[...]).astype(jnp.float32)

    def pick(k):
        rows = mod_ref[0, :, pl.ds(k, 1), :].reshape(prompts, -1)
        return lax.dot_general(
            onehot_t, rows, (((0,), (0,)), ((), ())),
            precision=lax.Precision.HIGHEST, preferred_element_type=jnp.float32,
        )

    shift, scale, gate = pick(0), pick(1), pick(2)
    xin_ref[...] = (normed * (1.0 + scale) + shift).astype(xin_ref.dtype)
    gate_ref[...] = gate


def exchange_kernel(src, tok_ref, ids_ref, mod_ref, dst, xin_ref, gate_ref, send_sem, recv_sem, local_sem):
    n = src.shape[0]
    n_y = 4
    n_zh = n // (2 * n_y)
    mc = lax.axis_index("mc")
    zh = lax.div(mc, n_y)
    yy = lax.rem(mc, n_y)
    c = lax.axis_index("core")
    me = mc * 2 + c
    r = lax.axis_index("rep")
    offsets = _offsets(n_zh, n_y)

    def peer(o, sign):
        z2 = lax.rem(zh + sign * o[0] + n_zh, n_zh)
        y2 = lax.rem(yy + sign * o[1] + n_y, n_y)
        c2 = lax.rem(c + sign * o[2] + 2, 2)
        return (z2 * n_y + y2) * 2 + c2, (r, z2 * n_y + y2, c2)

    barrier = pltpu.get_barrier_semaphore()
    for o in offsets:
        pl.semaphore_signal(barrier, 1, device_id=peer(o, 1)[1], device_id_type=MESH_ID)
    pl.semaphore_wait(barrier, n - 1)
    sends = []
    for j, o in enumerate(offsets):
        t, dev = peer(o, 1)
        cp = pltpu.make_async_remote_copy(
            src_ref=src.at[t],
            dst_ref=dst.at[me],
            send_sem=send_sem.at[j],
            recv_sem=recv_sem.at[j],
            device_id=dev,
            device_id_type=MESH_ID,
        )
        cp.start()
        sends.append(cp)
    own = pltpu.make_async_copy(src.at[me], dst.at[me], local_sem.at[0])
    own.start()
    modulate(tok_ref, ids_ref, mod_ref, xin_ref, gate_ref)
    for j, o in enumerate(offsets):
        s, dev = peer(o, -1)
        pltpu.make_async_remote_copy(
            src_ref=src.at[s],
            dst_ref=dst.at[s],
            send_sem=send_sem.at[j],
            recv_sem=recv_sem.at[j],
            device_id=dev,
            device_id_type=MESH_ID,
        ).wait_recv()
    for cp in sends:
        cp.wait_send()
    own.wait()


def exchange(pieces, tokens, ids, mod):
    n = pieces.shape[0]
    vmem = pl.BlockSpec(memory_space=pltpu.VMEM)
    return pl.pallas_call(
        exchange_kernel,
        out_shape=(
            jax.ShapeDtypeStruct(pieces.shape, pieces.dtype),
            jax.ShapeDtypeStruct(tokens.shape, jnp.bfloat16),
            jax.ShapeDtypeStruct(tokens.shape, jnp.float32),
        ),
        in_specs=[pl.BlockSpec(memory_space=pl.ANY), vmem, vmem, vmem],
        out_specs=(pl.BlockSpec(memory_space=pl.ANY), vmem, vmem),
        scratch_shapes=[
            pltpu.SemaphoreType.DMA((n,)),
            pltpu.SemaphoreType.DMA((n,)),
            pltpu.SemaphoreType.DMA((1,)),
        ],
        compiler_params=pltpu.CompilerParams(collective_id=1, has_side_effects=True),
    )(pieces, tokens, ids, mod)


def handover_kernel(up_ref, dn_ref, up_out, dn_out, send_sem, recv_sem, fwd_send, fwd_recv, local_sem):
    n_rep = up_out.shape[1]
    n_x = n_rep // 2
    me = lax.axis_index("rep")
    mc = lax.axis_index("mc")
    c = lax.axis_index("core")
    other = 1 - c
    x = lax.div(me, 2)
    zl = lax.rem(me, 2)
    partner = me + 1 - 2 * zl
    xs = [lax.rem(x + d, n_x) * 2 for d in range(1, n_x)]

    barrier = pltpu.get_barrier_semaphore()
    for t in [partner] + [xo + zl for xo in xs]:
        pl.semaphore_signal(barrier, 1, device_id=(t, mc, c), device_id_type=MESH_ID)
    pl.semaphore_signal(barrier, 1, device_id=(me, mc, other), device_id_type=MESH_ID)
    pl.semaphore_wait(barrier, n_x + 1)

    pairs = ((up_ref, up_out), (dn_ref, dn_out))

    def recv_desc(i, slot):
        dst = pairs[i][1]
        return pltpu.make_async_remote_copy(
            src_ref=dst.at[c, slot],
            dst_ref=dst.at[c, slot],
            send_sem=send_sem.at[i, 0],
            recv_sem=recv_sem.at[i, slot],
            device_id=(slot, mc, c),
            device_id_type=MESH_ID,
        )

    locals_ = []
    sends = []
    for i, (src, dst) in enumerate(pairs):
        cp = pltpu.make_async_copy(src, dst.at[c, me], local_sem.at[i])
        cp.start()
        locals_.append(cp)
        for j, t in enumerate([partner] + [xo + zl for xo in xs]):
            cp = pltpu.make_async_remote_copy(
                src_ref=src,
                dst_ref=dst.at[c, me],
                send_sem=send_sem.at[i, j],
                recv_sem=recv_sem.at[i, me],
                device_id=(t, mc, c),
                device_id_type=MESH_ID,
            )
            cp.start()
            sends.append(cp)
    for i, (src, dst) in enumerate(pairs):
        recv_desc(i, partner).wait_recv()
        for j, xo in enumerate(xs):
            cp = pltpu.make_async_remote_copy(
                src_ref=dst.at[c, partner],
                dst_ref=dst.at[c, partner],
                send_sem=send_sem.at[i, n_x + j],
                recv_sem=recv_sem.at[i, partner],
                device_id=(xo + zl, mc, c),
                device_id_type=MESH_ID,
            )
            cp.start()
            sends.append(cp)

    forwards = []
    for i, (src, dst) in enumerate(pairs):
        order = [me, partner] + [xo + zl for xo in xs] + [xo + 1 - zl for xo in xs]
        for slot in order:
            if slot is me:
                locals_[i].wait()
            elif slot is not partner:
                recv_desc(i, slot).wait_recv()
            fw = pltpu.make_async_remote_copy(
                src_ref=dst.at[c, slot],
                dst_ref=dst.at[c, slot],
                send_sem=fwd_send.at[i, slot],
                recv_sem=fwd_recv.at[i, slot],
                device_id=(me, mc, other),
                device_id_type=MESH_ID,
            )
            fw.start()
            forwards.append(fw)

    for cp in sends:
        cp.wait_send()
    for i, (src, dst) in enumerate(pairs):
        for slot in range(n_rep):
            pltpu.make_async_remote_copy(
                src_ref=dst.at[other, slot],
                dst_ref=dst.at[other, slot],
                send_sem=fwd_send.at[i, slot],
                recv_sem=fwd_recv.at[i, slot],
                device_id=(me, mc, other),
                device_id_type=MESH_ID,
            ).wait_recv()
    for fw in forwards:
        fw.wait_send()


def handover(up_blk, dn_blk, n_rep):
    units, width = up_blk.shape
    shape = jax.ShapeDtypeStruct((2, n_rep, units, width), up_blk.dtype)
    return pl.pallas_call(
        handover_kernel,
        out_shape=(shape, shape),
        in_specs=[pl.BlockSpec(memory_space=pl.ANY)] * 2,
        out_specs=(pl.BlockSpec(memory_space=pl.ANY),) * 2,
        scratch_shapes=[
            pltpu.SemaphoreType.DMA((2, n_rep)),
            pltpu.SemaphoreType.DMA((2, n_rep)),
            pltpu.SemaphoreType.DMA((2, n_rep)),
            pltpu.SemaphoreType.DMA((2, n_rep)),
            pltpu.SemaphoreType.DMA((2,)),
        ],
        compiler_params=pltpu.CompilerParams(collective_id=0, has_side_effects=True),
    )(up_blk, dn_blk)


def local(tokens, prompt_ids, modulation, trainer_up, trainer_down):
    as_float = tokens[0].astype(jnp.float32)
    n_mp = lax.psum(1, MP)
    n_rep = lax.psum(1, "rep")
    rows, cols = trainer_up.shape
    piece = cols // n_mp
    both = jnp.stack([trainer_up.astype(jnp.bfloat16).T, trainer_down.astype(jnp.bfloat16)])
    flat = (piece * rows // 120, 120)
    both, xin, gate = exchange(
        both.reshape(2, n_mp, *flat).transpose(1, 0, 2, 3), tokens[0], prompt_ids, modulation
    )
    x_all = lax.all_gather(xin, "mc", axis=0, tiled=True)
    both = both.reshape(n_mp, 2, piece, rows).transpose(1, 2, 0, 3)
    both = both.reshape(2, piece, n_mp * rows)
    up_all, dn_all = handover(both[0], both[1], n_rep)
    units = 2 * n_rep * piece
    w_up_t = up_all.reshape(units, n_mp * rows)
    w_down = dn_all.reshape(units, n_mp * rows)

    hidden = jax.nn.gelu(
        lax.dot_general(x_all, w_up_t, (((1,), (1,)), ((), ())), preferred_element_type=jnp.float32),
        approximate=True,
    ).astype(jnp.bfloat16)
    mlp = lax.psum_scatter(
        jnp.dot(hidden, w_down, preferred_element_type=jnp.float32).astype(jnp.bfloat16),
        "mc",
        scatter_dimension=0,
        tiled=True,
    ).astype(jnp.float32)
    result = as_float + gate * mlp
    return result.astype(jnp.bfloat16)[None]


def solution(mesh):
    n_rep, n_mp = mesh.devices.shape
    chips = Mesh(mesh.devices.reshape(n_rep, n_mp // 2, 2), ("rep", "mc", "core"))
    in_specs = (
        P("rep", MP, None),
        P("rep", MP),
        P("rep", None, None, None),
        P(MP, "rep"),
        P("rep", MP),
    )
    out_specs = P("rep", MP, None)
    return jax.shard_map(local, mesh=chips, in_specs=in_specs, out_specs=out_specs, check_vma=False)
```
